512 devices in a mesh: dp: 8 (over y, core), expert: 64 (over x, z).
Axes of the slice: x: 4, y: 4, z: 16, core: 2. Of those that a mesh axis runs over, the one named last changes fastest.
Arguments:
- tokens: bfloat16 [16384, 2048], P(('dp', 'expert')), may hold values from -6 to 6
- cotangent: bfloat16 [16384, 2048], P(('dp', 'expert')), may hold values from -0.29882812 to 0.29882812
- routes: int32 [16384, 8], P(('dp', 'expert')), may hold values from 0 to 63, all different within a row; in each aligned block of 32 rows (0 to 31, 32 to 63, ...) at most 8 rows name the same one
- combine: float32 [16384, 8], P(('dp', 'expert')), may hold values from 0.05 to 0.5
- w_in: bfloat16 [64, 2, 512, 2048], P('expert', None, 'dp'), may hold values from -0.125 to 0.125
- w_out: bfloat16 [64, 512, 2048], P('expert', 'dp'), may hold values from -0.25 to 0.25
- v_in: bfloat16 [64, 2, 512, 2048], P('expert', None, 'dp'), may hold values from -0.125 to 0.125
Outputs:
- hvp: float32 [64, 2, 512, 2048], P('expert', None, 'dp')
The draws below stay inside these ranges and needn't reach their ends.
Inputs may be any that keep to these rules, and one draw needn't show every extreme that they name: `routes`: each token names 8 different experts. Among the tokens of one device no expert is named more than 8 times, and on some device an expert is named exactly 8 times.
All inputs are finite; a program needn't handle non-finite values.
Results may differ from the reference program's by a relative error of at most 0.015.
Values may be sent and summed in bfloat16 or wider, within the bound.
A program may use at most 128 MiB of HBM per device.

```python
import math
import jax
import jax.numpy as jnp
import numpy as np
from jax import lax

D = 2048
TOP = 8
FF_W = 512
TOK_DEV = 32
EXPERTS = 64
TOKENS = 16384
CAP = 8
N_DP = 8
N_EXPERT = 64


def steps_of(rng, dims, shards, smallest, top_value):
    level = 1.0
    for dim, blocks in shards:
        steps = jax.random.uniform(jax.random.fold_in(jax.random.fold_in(rng, 6), dim), (blocks,), jnp.float32, smallest / len(shards), top_value / len(shards))
        level = level * jnp.repeat(jnp.exp(steps), dims[dim] // blocks).reshape((-1,) + (1,) * (len(dims) - 1 - dim))
    return level


def deal_out(key, own, number, rows, count, top, bound, slope):
    order = jax.random.permutation(key, count)
    crowded, common = shares(count, rows * top, bound, slope, True), shares(count, rows * top, bound, slope, False)
    places = jnp.arange(count)

    def named(sizes, offset_by):
        used = int((sizes > 0).sum())
        fixed = max(1, used // 4)
        moved = fixed + (places - fixed + offset_by * (used - fixed)) % max(1, count - fixed)
        return jnp.zeros((count,), jnp.int32).at[order[jnp.where(places < fixed, places, moved)]].set(jnp.asarray(sizes, jnp.int32))

    sizes = jnp.where(number % 4 == 0, named(crowded, number // 4), named(common, number - number // 4 - 1))
    mixed = jax.random.permutation(jax.random.fold_in(own, 3), count)
    giver, taker = mixed[0:count // 2 * 2:2], mixed[1:count // 2 * 2:2]
    room = jnp.minimum(sizes[giver] - 1, bound - sizes[taker]) // 2
    room = jnp.where((giver == order[0]) | (taker == order[0]) | (sizes[taker] == 0), 0, jnp.maximum(room, 0))
    moved = jax.random.randint(jax.random.fold_in(own, 4), (count // 2,), 0, 1 << 20) % (room + 1)
    sizes = sizes.at[giver].add(-moved).at[taker].add(moved)
    members = jnp.searchsorted(jnp.cumsum(sizes), jnp.arange(rows * top), side="right").astype(jnp.int32)
    listing = members.reshape(top, rows).T
    listing = listing[jax.random.permutation(jax.random.fold_in(own, 1), rows)]
    offset_by = jax.random.randint(jax.random.fold_in(own, 2), (rows, 1), 0, top)
    return jnp.take_along_axis(listing, (jnp.arange(top)[None, :] + offset_by) % top, axis=1)


def shares(amount, total, reach, skew, full):
    portions = [(1 << 20) // math.isqrt(rank ** skew) + 1 for rank in range(1, amount + 1)]
    largest = reach if full else min(reach, max(-(-total // amount), total * portions[0] // sum(portions)))
    least = 1 if total - largest >= amount - 1 else 0
    counts, surplus = [largest] + [least] * (amount - 1), total - largest - least * (amount - 1)
    while surplus > 0:
        movable = [i for i in range(1, amount) if counts[i] < largest] or [i for i in range(1, amount) if counts[i] < reach]
        whole, budget = sum([portions[i] for i in movable]), surplus
        for i in movable:
            addition = min(reach - counts[i], max(1, budget * portions[i] // whole), surplus)
            counts[i] = counts[i] + addition
            surplus = surplus - addition
    return np.array(counts)


def noise(rng, shape, width, most, cuts=(), kind=jnp.bfloat16):
    loudness = steps_of(rng, shape, cuts, -0.22, 0.18) if cuts else 1.0
    values = jax.random.normal(rng, shape, jnp.float32) * width * loudness
    return jnp.minimum(jnp.maximum(values, -most), most).astype(kind)


def setup_inputs(seed: int = 0) -> dict:
    streams_of = jax.random.split(jax.random.key(seed), 8)
    tokens = noise(streams_of[0], (TOKENS, D), 1.0, 6.0, ((0, 512),))
    cotangent = noise(streams_of[1], (TOKENS, D), 0.05, 0.29882812, ((0, 512),))
    routes_keys = jax.random.split(jax.random.fold_in(streams_of[2], 1), TOKENS // TOK_DEV)
    routes_turns = jax.random.permutation(jax.random.fold_in(streams_of[2], 3), TOKENS // TOK_DEV)
    routes = jax.vmap(lambda own, number: deal_out(jax.random.fold_in(streams_of[2], 2), own, number, TOK_DEV, EXPERTS, TOP, CAP, 2))(routes_keys, routes_turns).reshape((TOKENS, TOP))
    combine = jnp.clip(jnp.exp(math.log(0.5) - 2.3025851 * jax.random.uniform(streams_of[3], (TOKENS, TOP), jnp.float32) ** steps_of(streams_of[3], (TOKENS, TOP), ((0, 512),), -0.2, 0.2)), 0.05, 0.5)
    w_in = noise(streams_of[4], (EXPERTS, 2, FF_W, D), D ** -0.5, 0.125, ((0, 64), (2, 8)))
    w_out = noise(streams_of[5], (EXPERTS, FF_W, D), FF_W ** -0.5, 0.25, ((0, 64), (1, 8)))
    v_in = noise(streams_of[6], (EXPERTS, 2, FF_W, D), D ** -0.5, 0.125, ((0, 64), (2, 8)))
    return {"tokens": tokens, "cotangent": cotangent, "routes": routes, "combine": combine, "w_in": w_in, "w_out": w_out, "v_in": v_in}


def expert_terms(slot_rows, slot_grads, w_pair, v_pair, w_down):
    hidden_width = w_pair.shape[1]
    model_dim = w_pair.shape[2]
    stacked = jnp.concatenate([w_pair, v_pair], axis=0).reshape(4 * hidden_width, model_dim)
    projected = lax.dot_general(slot_rows, stacked, (((1,), (1,)), ((), ())), preferred_element_type=jnp.float32)
    pre_gate = projected[:, :hidden_width]
    pre_up = projected[:, hidden_width:2 * hidden_width]
    tan_gate = projected[:, 2 * hidden_width:3 * hidden_width]
    tan_up = projected[:, 3 * hidden_width:]
    back_grad = lax.dot_general(slot_grads, w_down, (((1,), (1,)), ((), ())), preferred_element_type=jnp.float32)
    gate_sig = jax.nn.sigmoid(pre_gate)
    first_deriv = gate_sig * (1.0 + pre_gate * (1.0 - gate_sig))
    second_deriv = gate_sig * (1.0 - gate_sig) * (2.0 + pre_gate * (1.0 - 2.0 * gate_sig))
    gate_dir = (back_grad * (tan_up * first_deriv + pre_up * second_deriv * tan_gate)).astype(jnp.bfloat16)
    up_dir = (back_grad * first_deriv * tan_gate).astype(jnp.bfloat16)
    gate_term = lax.dot_general(gate_dir, slot_rows, (((0,), (0,)), ((), ())), preferred_element_type=jnp.float32)
    up_term = lax.dot_general(up_dir, slot_rows, (((0,), (0,)), ((), ())), preferred_element_type=jnp.float32)
    return jnp.stack([gate_term, up_term], axis=0)


def reference(tokens, cotangent, routes, combine, w_in, w_out, v_in):
    pair_count = TOK_DEV * TOP
    per_group = N_EXPERT * TOK_DEV
    slot_count = N_EXPERT * CAP
    grouped = routes.reshape(N_DP, N_EXPERT, pair_count)
    onehot = (grouped[..., None] == jnp.arange(EXPERTS, dtype=jnp.int32)).astype(jnp.int32)
    earlier = jnp.cumsum(onehot, axis=2) - onehot
    slot_rank = jnp.sum(earlier * onehot, axis=3)
    source = jnp.arange(N_EXPERT, dtype=jnp.int32)[None, :, None]
    position = (grouped * slot_count + source * CAP + slot_rank).astype(jnp.int32)
    pair_id = jnp.broadcast_to(source * pair_count + jnp.arange(pair_count, dtype=jnp.int32)[None, None, :], position.shape).astype(jnp.int32)
    group_id = jnp.broadcast_to(jnp.arange(N_DP, dtype=jnp.int32)[:, None, None], position.shape)
    slot_table = jnp.full((N_DP, EXPERTS * slot_count), per_group * TOP, jnp.int32)
    slot_table = slot_table.at[group_id, position].set(pair_id)
    slot_table = slot_table.reshape(N_DP, EXPERTS, slot_count)
    tok_pad = jnp.concatenate([tokens.reshape(N_DP, per_group, D), jnp.zeros((N_DP, 1, D), tokens.dtype)], axis=1)
    cot_pad = jnp.concatenate([cotangent.reshape(N_DP, per_group, D), jnp.zeros((N_DP, 1, D), cotangent.dtype)], axis=1)
    comb_pad = jnp.concatenate([combine.reshape(N_DP, per_group, TOP), jnp.zeros((N_DP, 1, TOP), combine.dtype)], axis=1)

    def one_expert(expert):
        def one_group(running_sum, group):
            entries = slot_table[group, expert]
            token_index = entries // TOP
            choice_index = entries % TOP
            slot_rows = tok_pad[group][token_index]
            weight_col = comb_pad[group][token_index, choice_index]
            slot_grads = (weight_col[:, None] * cot_pad[group][token_index].astype(jnp.float32)).astype(jnp.bfloat16)
            partial_value = expert_terms(slot_rows, slot_grads, w_in[expert], v_in[expert], w_out[expert])
            rounded = lax.optimization_barrier(partial_value.astype(jnp.bfloat16))
            return running_sum + rounded.astype(jnp.float32), None

        zero_start = jnp.zeros((2, FF_W, D), jnp.float32)
        result, _ = lax.scan(one_group, zero_start, jnp.arange(N_DP, dtype=jnp.int32))
        return result

    return lax.map(one_expert, jnp.arange(EXPERTS, dtype=jnp.int32))
```

```python
import functools

import jax
import jax.numpy as jnp
from jax import lax
from jax.experimental import pallas as pl
from jax.experimental.pallas import tpu as pltpu
from jax.sharding import PartitionSpec as P

MESH = pl.DeviceIdType.MESH
F32 = jnp.float32
BF16 = jnp.bfloat16
NX = 4
NY = 4
NC = 2
CAP = 8
QFAR, QNEXT, QPREV, QOWN = 0, 1, 2, 3


def kernel(
    nz, tok_hbm, cot_hbm, routes_ref, combine_ref, win_hbm, wout_hbm, vin_hbm, out_ref,
    zx, zc, zm, sx, sg, lx, lg, rx, rg, wbuf, proj, dirs, hold, sb, rb,
    loc_sem, zs_sem, zr_sem, ys_sem, yr_sem, xs_sem, xr_sem, xl_sem, ps_sem, pr_sem, rs_sem, rr_sem,
):
    steps = nz // 2
    groups = steps
    last = groups - 1
    tok_dev, dim = tok_hbm.shape
    top = routes_ref.shape[1]
    hs = wout_hbm.shape[1]
    dp = lax.axis_index("dp")
    ex = lax.axis_index("expert")
    y, core = dp // NC, dp % NC
    x, z = ex // nz, ex % nz

    def at_z(k):
        return (dp, x * nz + (z + k + nz) % nz)

    def at_x(k):
        return (dp, ((x + k + NX) % NX) * nz + z)

    def at_y(k):
        return (((y + k + NY) % NY) * NC + core, ex)

    partner = (y * NC + (1 - core), ex)

    local = [
        pltpu.make_async_copy(tok_hbm, zx.at[last, 0], loc_sem.at[0]),
        pltpu.make_async_copy(cot_hbm, zc.at[last, 0], loc_sem.at[1]),
        pltpu.make_async_copy(win_hbm.at[0], wbuf.at[pl.ds(0, 2), QOWN], loc_sem.at[2]),
        pltpu.make_async_copy(vin_hbm.at[0], wbuf.at[pl.ds(2, 2), QOWN], loc_sem.at[3]),
        pltpu.make_async_copy(wout_hbm.at[0], wbuf.at[4, QOWN], loc_sem.at[4]),
    ]
    for c in local:
        c.start()

    barrier = pltpu.get_barrier_semaphore()
    neighbours = [at_z(1), at_z(-1), at_x(1), at_x(-1), at_y(1), at_y(-1), partner]
    for n in neighbours:
        pl.semaphore_signal(barrier, inc=1, device_id=n, device_id_type=MESH)
    pl.semaphore_wait(barrier, len(neighbours))

    sent = []

    def send(src, dst, ssem, rsem, device):
        c = pltpu.make_async_remote_copy(
            src_ref=src, dst_ref=dst, send_sem=ssem, recv_sem=rsem, device_id=device, device_id_type=MESH
        )
        c.start()
        sent.append(c)
        return c

    zbuf = (zx, zc, zm)

    def z_send(way, kind, s):
        src = (last, 0) if s == 1 else (s - 2, way)
        dst = (s - 1, way) if s < steps else (last, 1)
        buf = zbuf[kind]
        return send(
            buf.at[src], buf.at[dst], zs_sem.at[way, kind, s - 1], zr_sem.at[way, kind, s - 1],
            at_z(1 if way == 0 else -1),
        )

    def z_lanes(s):
        lanes = [(0, 0), (1, 0), (0, 1), (1, 1), (0, 2), (1, 2)]
        if s < steps:
            return lanes
        return [(0, 0), (1, 1), (0, 2)]

    zcp = {}
    local[0].wait()
    local[1].wait()
    for way, kind in z_lanes(1):
        if kind < 2:
            zcp[way, kind, 1] = z_send(way, kind, 1)

    half_rows = hs // 2

    def piece(q, i):
        if i == 0:
            return wbuf.at[pl.ds(0, 2), q]
        if i == 1:
            return wbuf.at[4, q, pl.ds(0, half_rows)]
        if i == 2:
            return wbuf.at[pl.ds(2, 2), q]
        return wbuf.at[4, q, pl.ds(half_rows, half_rows)]

    for c in local[2:]:
        c.wait()
    ycp = {}
    for n in range(4):
        for way in (0, 1):
            i = n if way == 0 else (n + 2) % 4
            ycp[way, i] = send(
                piece(QOWN, i), piece(QPREV if way == 0 else QNEXT, i),
                ys_sem.at[way, i], yr_sem.at[way, i], at_y(1 if way == 0 else -1),
            )

    def y_forward():
        for n in range(2):
            for way in (0, 1):
                i = n if way == 0 else n + 2
                ycp[way, i].wait_recv()
                ycp[way, 4 + n] = send(
                    piece(QPREV if way == 0 else QNEXT, i), piece(QFAR, i),
                    ys_sem.at[way, 4 + n], yr_sem.at[way, 4 + n], at_y(1 if way == 0 else -1),
                )

    def y_finish():
        for way in (0, 1):
            for n in range(2):
                ycp[way, (n + 2) % 4 if way == 0 else n].wait_recv()
        for way in (0, 1):
            for n in range(2):
                ycp[way, 4 + n].wait_recv()

    routes = routes_ref[...]
    combine = combine_ref[...]
    lane = lax.broadcasted_iota(jnp.int32, (tok_dev, 128), 1)
    token_f = lax.broadcasted_iota(jnp.int32, (tok_dev, 128), 0).astype(F32)
    slot_f = (lane % CAP).astype(F32)
    expert_x = ((lane % 64) // 16) * nz
    earlier = (
        lax.broadcasted_iota(jnp.int32, (tok_dev, tok_dev), 1)
        < lax.broadcasted_iota(jnp.int32, (tok_dev, tok_dev), 0)
    )
    earlier = jnp.where(earlier, 1.0, 0.0).astype(BF16)

    def table_row(zz, carry):
        wanted = expert_x + zz
        member = jnp.zeros((tok_dev, 128), F32)
        weight = jnp.zeros((tok_dev, 128), F32)
        for k in range(top):
            hit = routes[:, k : k + 1] == wanted
            member = member + jnp.where(hit, 1.0, 0.0)
            weight = weight + jnp.where(hit, combine[:, k : k + 1], 0.0)
        rank = jnp.dot(earlier, member.astype(BF16), preferred_element_type=F32)
        chosen = jnp.where(rank == slot_f, member, 0.0)
        index_row = jnp.sum(chosen * (token_f + 1.0), axis=0, keepdims=True) - 1.0
        weight_row = jnp.sum(chosen * weight, axis=0, keepdims=True)
        zm[last, 0, pl.ds(zz, 1), :] = jnp.where(lane[:1] < 64, index_row, weight_row)
        return carry

    lax.fori_loop(0, nz, table_row, 0)
    for way, kind in z_lanes(1):
        if kind == 2:
            zcp[way, kind, 1] = z_send(way, kind, 1)

    srow = lax.broadcasted_iota(jnp.int32, (64, 128), 0)
    slane = lax.broadcasted_iota(jnp.int32, (64, 128), 1)
    upper = ((srow[:, :1] // 8) % 2).astype(F32)
    pick_lane = lax.broadcasted_iota(jnp.int32, (64, 2 * tok_dev), 1).astype(F32)
    chunk = min(512, dim)
    chunks = dim // chunk

    def select(p):
        ma = zm[p, 0, pl.ds(z, 1), :]
        mb = zm[p, 1, pl.ds(z, 1), :]
        m = jnp.where((slane[:1] // 8) % 2 == 0, ma, mb)
        m = jnp.broadcast_to(m, (64, 128))
        index_col = jnp.sum(jnp.where(slane == srow, m, 0.0), axis=1, keepdims=True)
        weight_col = jnp.sum(jnp.where(slane == srow + 64, m, 0.0), axis=1, keepdims=True)
        index_col = jnp.where(index_col >= 0.0, index_col + upper * tok_dev, -1.0)
        pick = jnp.where(index_col == pick_lane, 1.0, 0.0).astype(BF16)

        def body(n, carry):
            cols = pl.ds(pl.multiple_of(n * chunk, chunk), chunk)
            rows = zx[p, :, :, cols].reshape(2 * tok_dev, chunk)
            got = jnp.dot(pick, rows, preferred_element_type=F32).astype(BF16)
            sx[p, :, :, cols] = got.reshape(NX, 16, chunk)
            grads = zc[p, :, :, cols].reshape(2 * tok_dev, chunk)
            got = (weight_col * jnp.dot(pick, grads, preferred_element_type=F32)).astype(BF16)
            sg[p, :, :, cols] = got.reshape(NX, 16, chunk)
            return carry

        lax.fori_loop(0, chunks, body, 0)

    xcp = {}
    x_far, x_next, x_prev = (x + 2) % NX, (x + 1) % NX, (x + 3) % NX

    def x_send(p):
        def one(i, src, dst, way):
            xcp[i, p] = send(src, dst, xs_sem.at[i, p], xr_sem.at[i, p], at_x(way))

        one(0, sx.at[p, x_far], lx.at[p], 1)
        one(1, sg.at[p, x_far], lg.at[p], -1)
        one(2, sx.at[p, x_next], rx.at[p, 0, 1], 1)
        one(3, sx.at[p, x_prev], rx.at[p, 0, 3], -1)
        one(4, sg.at[p, x_next], rg.at[p, 0, 1], 1)
        one(5, sg.at[p, x_prev], rg.at[p, 0, 3], -1)
        for i, (s, d) in enumerate(((sx, rx), (sg, rg))):
            c = pltpu.make_async_copy(s.at[p, x], d.at[p, 0, 0], xl_sem.at[i, p])
            c.start()
            xcp[8 + i, p] = c

    def x_relay(p):
        xcp[0, p].wait_recv()
        xcp[6, p] = send(lx.at[p], rx.at[p, 0, 2], xs_sem.at[6, p], xr_sem.at[6, p], at_x(1))
        xcp[1, p].wait_recv()
        xcp[7, p] = send(lg.at[p], rg.at[p, 0, 2], xs_sem.at[7, p], xr_sem.at[7, p], at_x(-1))

    pcp = {}

    def to_partner(p):
        xcp[8, p].wait()
        for i in (2, 3, 6):
            xcp[i, p].wait_recv()
        pcp[0, p] = send(rx.at[p, 0], rx.at[p, 1], ps_sem.at[0, p], pr_sem.at[0, p], partner)
        xcp[9, p].wait()
        for i in (4, 5, 7):
            xcp[i, p].wait_recv()
        pcp[1, p] = send(rg.at[p, 0], rg.at[p, 1], ps_sem.at[1, p], pr_sem.at[1, p], partner)

    span = 4 * 2 * NX * 16 // 2
    hidden = 4 * hs

    def terms(b):
        def project(k, carry):
            rows = rx[2 * b : 2 * b + 2].reshape(span, dim)
            proj[k] = lax.dot_general(
                wbuf[k].reshape(hidden, dim), rows, (((1,), (1,)), ((), ())), preferred_element_type=F32
            )
            return carry

        for i in (0, 1):
            for p in (2 * b, 2 * b + 1):
                pcp[i, p].wait_recv()
        lax.fori_loop(0, 4, project, 0)
        proj[4] = lax.dot_general(
            wbuf[4].reshape(hidden, dim), rg[2 * b : 2 * b + 2].reshape(span, dim),
            (((1,), (1,)), ((), ())), preferred_element_type=F32,
        )

        def pointwise(i, carry):
            rows = pl.ds(pl.multiple_of(i * 32, 32), 32)
            pre_gate, pre_up, tan_gate, tan_up, back = [proj[k, rows, :] for k in range(5)]
            sig = 1.0 / (1.0 + jnp.exp(-pre_gate))
            first = sig * (1.0 + pre_gate * (1.0 - sig))
            second = sig * (1.0 - sig) * (2.0 + pre_gate * (1.0 - 2.0 * sig))
            out_rows = pl.ds(pl.multiple_of((i % 4) * 32, 32), 32)
            cols = pl.ds(b * span, span)
            dirs[i // 4, 0, out_rows, cols] = (back * (tan_up * first + pre_up * second * tan_gate)).astype(BF16)
            dirs[i // 4, 1, out_rows, cols] = (back * first * tan_gate).astype(BF16)
            return carry

        lax.fori_loop(0, hidden // 32, pointwise, 0)

    def group_of(s):
        return s - 1

    for s in range(1, steps + 1):
        for way, kind in z_lanes(s):
            zcp[way, kind, s].wait_recv()
            if s < steps and (way, kind) in z_lanes(s + 1):
                zcp[way, kind, s + 1] = z_send(way, kind, s + 1)
        select(group_of(s))
        x_send(group_of(s))
        if s >= 2:
            x_relay(group_of(s - 1))
        if s >= 3:
            to_partner(group_of(s - 2))
        if s == 3:
            y_forward()
    y_finish()
    terms(0)
    to_partner(last - 1)
    terms(1)
    x_relay(last)
    terms(2)
    to_partner(last)
    terms(3)

    def product(h):
        def body(n, carry):
            cols = pl.ds(pl.multiple_of(n * chunk, chunk), chunk)
            rows = rx[:, :, :, :, cols].reshape(groups * 2 * NX * 16, chunk)
            acc = jnp.dot(dirs[h].reshape(4 * hs, groups * 2 * NX * 16), rows, preferred_element_type=F32)
            if h == 0:
                sb[0, :, cols] = acc[:hs].astype(BF16)
                hold[0, :, cols] = acc[hs : 2 * hs]
                sb[1, :, cols] = acc[2 * hs : 3 * hs].astype(BF16)
                sb[2, :, cols] = acc[3 * hs :].astype(BF16)
            else:
                sb[3, :, cols] = acc[:hs].astype(BF16)
                out_ref[0, 0, :, cols] = acc[hs : 2 * hs]
                hold[1, :, cols] = acc[2 * hs : 3 * hs]
                out_ref[0, 1, :, cols] = acc[3 * hs :]
            return carry

        lax.fori_loop(0, chunks, body, 0)

    rcp = {}

    def r_send(i, src, way):
        rcp[i] = send(sb.at[src], rb.at[i], rs_sem.at[i], rr_sem.at[i], at_y(way))

    product(0)
    r_send(0, 0, 1)
    r_send(1, 1, -1)
    r_send(2, 2, 1)
    product(1)
    r_send(3, 3, -1)
    rcp[0].wait_recv()
    sb[4] = (hold[0] + rb[0].astype(F32)).astype(BF16)
    r_send(4, 4, 1)
    rcp[1].wait_recv()
    sb[5] = (hold[1] + rb[1].astype(F32)).astype(BF16)
    r_send(5, 5, -1)
    rcp[2].wait_recv()
    out_ref[0, 1] += rb[2].astype(F32)
    rcp[3].wait_recv()
    out_ref[0, 0] += rb[3].astype(F32)
    rcp[4].wait_recv()
    out_ref[0, 0] += rb[4].astype(F32)
    rcp[5].wait_recv()
    out_ref[0, 1] += rb[5].astype(F32)
    for c in sent:
        c.wait_send()


def local(tokens, cotangent, routes, combine, w_in, w_out, v_in):
    nz = lax.axis_size("expert") // NX
    groups = nz // 2
    tok_dev, dim = tokens.shape
    hs = w_out.shape[1]
    span = 2 * 2 * NX * 16
    any_spec = pl.BlockSpec(memory_space=pl.ANY)
    vmem_spec = pl.BlockSpec(memory_space=pltpu.VMEM)
    dma = pltpu.SemaphoreType.DMA
    return pl.pallas_call(
        functools.partial(kernel, nz),
        out_shape=jax.ShapeDtypeStruct((1, 2, hs, dim), F32),
        in_specs=[any_spec, any_spec, vmem_spec, vmem_spec, any_spec, any_spec, any_spec],
        out_specs=vmem_spec,
        scratch_shapes=[
            pltpu.VMEM((groups, 2, tok_dev, dim), BF16),
            pltpu.VMEM((groups, 2, tok_dev, dim), BF16),
            pltpu.VMEM((groups, 2, nz, 128), F32),
            pltpu.VMEM((groups, NX, 16, dim), BF16),
            pltpu.VMEM((groups, NX, 16, dim), BF16),
            pltpu.VMEM((groups, 16, dim), BF16),
            pltpu.VMEM((groups, 16, dim), BF16),
            pltpu.VMEM((groups, 2, NX, 16, dim), BF16),
            pltpu.VMEM((groups, 2, NX, 16, dim), BF16),
            pltpu.VMEM((5, 4, hs, dim), BF16),
            pltpu.VMEM((5, 4 * hs, span), F32),
            pltpu.VMEM((2, 2, 2 * hs, groups * 2 * NX * 16), BF16),
            pltpu.VMEM((2, hs, dim), F32),
            pltpu.VMEM((6, hs, dim), BF16),
            pltpu.VMEM((6, hs, dim), BF16),
            dma((5,)),
            dma((2, 3, groups)),
            dma((2, 3, groups)),
            dma((2, 6)),
            dma((2, 6)),
            dma((8, groups)),
            dma((8, groups)),
            dma((2, groups)),
            dma((2, groups)),
            dma((2, groups)),
            dma((6,)),
            dma((6,)),
        ],
        compiler_params=pltpu.CompilerParams(
            collective_id=0, has_side_effects=True, vmem_limit_bytes=60 * 1024 * 1024
        ),
    )(tokens, cotangent, routes, combine, w_in, w_out, v_in)


def solution(mesh):
    in_specs = (
        P(("dp", "expert"), None),
        P(("dp", "expert"), None),
        P(("dp", "expert"), None),
        P(("dp", "expert"), None),
        P("expert", None, "dp", None),
        P("expert", "dp", None),
        P("expert", None, "dp", None),
    )
    out_specs = P("expert", None, "dp", None)
    return jax.shard_map(local, mesh=mesh, in_specs=in_specs, out_specs=out_specs, check_vma=False)
```

```python
import functools

import jax
import jax.numpy as jnp
from jax import lax
from jax.experimental import pallas as pl
from jax.experimental.pallas import tpu as pltpu
from jax.sharding import PartitionSpec as P

MESH = pl.DeviceIdType.MESH
F32 = jnp.float32
BF16 = jnp.bfloat16
NX = 4
NY = 4
NC = 2
CAP = 8
QFAR, QNEXT, QPREV, QOWN = 0, 1, 2, 3


def kernel(
    nz, tok_hbm, cot_hbm, routes_ref, combine_ref, win_hbm, wout_hbm, vin_hbm, out_ref,
    zx, zc, zm, sx, sg, lx, lg, rx, rg, wbuf, proj, dirs, part, sb, rb,
    loc_sem, zs_sem, zr_sem, ys_sem, yr_sem, xs_sem, xr_sem, xl_sem, ps_sem, pr_sem, rs_sem, rr_sem,
):
    steps = nz // 2
    pairs = steps - 1
    own, far = 0, pairs + 1
    tok_dev, dim = tok_hbm.shape
    top = routes_ref.shape[0]
    hs = wout_hbm.shape[1]
    rows_of = 2 * NX * 16
    dp = lax.axis_index("dp")
    ex = lax.axis_index("expert")
    y, core = dp // NC, dp % NC
    x, z = ex // nz, ex % nz

    def at_z(k):
        return (dp, x * nz + (z + k + nz) % nz)

    def at_x(k):
        return (dp, ((x + k + NX) % NX) * nz + z)

    def at_y(k):
        return (((y + k + NY) % NY) * NC + core, ex)

    partner = (y * NC + (1 - core), ex)

    barrier = pltpu.get_barrier_semaphore()
    neighbours = [at_z(1), at_z(-1), at_x(1), at_x(-1), at_y(1), at_y(-1), partner]
    for n in neighbours:
        pl.semaphore_signal(barrier, inc=1, device_id=n, device_id_type=MESH)

    local = [
        pltpu.make_async_copy(tok_hbm, zx.at[pairs, 0], loc_sem.at[0]),
        pltpu.make_async_copy(cot_hbm, zc.at[pairs, 0], loc_sem.at[1]),
        pltpu.make_async_copy(win_hbm.at[0], wbuf.at[QOWN, pl.ds(0, 2)], loc_sem.at[2]),
        pltpu.make_async_copy(vin_hbm.at[0], wbuf.at[QOWN, pl.ds(2, 2)], loc_sem.at[3]),
        pltpu.make_async_copy(wout_hbm.at[0], wbuf.at[QOWN, 4], loc_sem.at[4]),
    ]
    for c in local:
        c.start()
    pl.semaphore_wait(barrier, len(neighbours))

    sent = []

    def send(src, dst, ssem, rsem, device):
        c = pltpu.make_async_remote_copy(
            src_ref=src, dst_ref=dst, send_sem=ssem, recv_sem=rsem, device_id=device, device_id_type=MESH
        )
        c.start()
        sent.append(c)
        return c

    zbuf = (zx, zc, zm)

    def z_send(way, kind, s):
        dst = (s - 1, way) if s < steps else (pairs, 1)
        buf = zbuf[kind]
        if s > 1:
            src = buf.at[s - 2, way]
        elif kind == 2:
            src = buf.at[pairs, 0]
        else:
            src = (tok_hbm, cot_hbm)[kind]
        return send(
            src, buf.at[dst], zs_sem.at[way, kind, s - 1], zr_sem.at[way, kind, s - 1],
            at_z(1 if way == 0 else -1),
        )

    def z_lanes(s):
        lanes = [(0, 0), (1, 0), (0, 1), (1, 1), (0, 2), (1, 2)]
        if s < steps:
            return lanes
        return [(0, 0), (1, 1), (0, 2)]

    zcp = {}
    for way, kind in z_lanes(1):
        if kind < 2:
            zcp[way, kind, 1] = z_send(way, kind, 1)

    half_rows = hs // 2

    def piece(q, i):
        if i == 0:
            return wbuf.at[q, pl.ds(0, 2)]
        if i == 1:
            return wbuf.at[q, 4, pl.ds(0, half_rows)]
        if i == 2:
            return wbuf.at[q, pl.ds(2, 2)]
        return wbuf.at[q, 4, pl.ds(half_rows, half_rows)]

    own_piece = (
        win_hbm.at[0], wout_hbm.at[0, pl.ds(0, half_rows)], vin_hbm.at[0], wout_hbm.at[0, pl.ds(half_rows, half_rows)]
    )
    ycp = {}
    for n in range(4):
        for way in (0, 1):
            i = n if way == 0 else (n + 2) % 4
            ycp[way, i] = send(
                own_piece[i], piece(QPREV if way == 0 else QNEXT, i),
                ys_sem.at[way, i], yr_sem.at[way, i], at_y(1 if way == 0 else -1),
            )

    def y_forward():
        for n in range(2):
            for way in (0, 1):
                i = n if way == 0 else n + 2
                ycp[way, i].wait_recv()
                ycp[way, 4 + n] = send(
                    piece(QPREV if way == 0 else QNEXT, i), piece(QFAR, i),
                    ys_sem.at[way, 4 + n], yr_sem.at[way, 4 + n], at_y(1 if way == 0 else -1),
                )

    def y_near():
        for c in local[2:]:
            c.wait()
        for way in (0, 1):
            for n in range(2):
                ycp[way, (n + 2) % 4 if way == 0 else n].wait_recv()

    def y_finish():
        for way in (0, 1):
            for n in range(2):
                ycp[way, 4 + n].wait_recv()

    lane = lax.broadcasted_iota(jnp.int32, (tok_dev, 128), 1)
    token_i = lax.broadcasted_iota(jnp.int32, (tok_dev, tok_dev), 0)
    token_j = lax.broadcasted_iota(jnp.int32, (tok_dev, tok_dev), 1)
    token_f = lax.broadcasted_iota(jnp.int32, (tok_dev, 128), 0).astype(F32)
    slot_f = (lane % CAP).astype(F32)
    expert_x = ((lane % 64) // 16) * nz
    earlier = jnp.where(token_j < token_i, 1.0, 0.0).astype(BF16)

    def column(row):
        picked = jnp.where(token_i == token_j, jnp.broadcast_to(row, (tok_dev, tok_dev)), 0.0)
        return jnp.broadcast_to(jnp.sum(picked, axis=1, keepdims=True), (tok_dev, 128))

    routes = [column(routes_ref[k : k + 1, :].astype(F32)) for k in range(top)]
    combine = [column(combine_ref[k : k + 1, :]) for k in range(top)]

    def table_row(zz, carry):
        wanted = (expert_x + zz).astype(F32)
        member = jnp.zeros((tok_dev, 128), F32)
        weight = jnp.zeros((tok_dev, 128), F32)
        for k in range(top):
            hit = routes[k] == wanted
            member = jnp.where(hit, 1.0, member)
            weight = jnp.where(hit, combine[k], weight)
        rank = jnp.dot(earlier, member.astype(BF16), preferred_element_type=F32)
        chosen = jnp.where(rank == slot_f, member, 0.0)
        value = jnp.where(lane < 64, token_f + 1.0, weight)
        total = jnp.sum(chosen * value, axis=0, keepdims=True)
        zm[pairs, 0, pl.ds(zz, 1), :] = jnp.where(lane[:1] < 64, total - 1.0, total)
        return carry

    lax.fori_loop(0, nz, table_row, 0)
    for way, kind in z_lanes(1):
        if kind == 2:
            zcp[way, kind, 1] = z_send(way, kind, 1)

    srow = lax.broadcasted_iota(jnp.int32, (64, 128), 0)
    slane = lax.broadcasted_iota(jnp.int32, (64, 128), 1)
    upper = ((srow[:, :1] // 8) % 2).astype(F32)
    chunk = min(512, dim)
    chunks = dim // chunk

    def columns_of(m):
        m = jnp.broadcast_to(m, (64, 128))
        index_col = jnp.sum(jnp.where(slane == srow, m, 0.0), axis=1, keepdims=True)
        weight_col = jnp.sum(jnp.where(slane == srow + 64, m, 0.0), axis=1, keepdims=True)
        return index_col, weight_col

    def one_hot(index_col, width):
        tokens = lax.broadcasted_iota(jnp.int32, (64, width), 1).astype(F32)
        return jnp.where(index_col == tokens, 1.0, 0.0).astype(BF16)

    def select(g):
        p = g - 1
        ma = zm[p, 0, pl.ds(z, 1), :]
        mb = zm[p, 1, pl.ds(z, 1), :]
        index_col, weight_col = columns_of(jnp.where((slane[:1] // 8) % 2 == 0, ma, mb))
        index_col = jnp.where(index_col >= 0.0, index_col + upper * tok_dev, -1.0)
        pick = one_hot(index_col, 2 * tok_dev)

        def body(n, carry):
            cols = pl.ds(pl.multiple_of(n * chunk, chunk), chunk)
            rows = zx[p, :, :, cols].reshape(2 * tok_dev, chunk)
            got = jnp.dot(pick, rows, preferred_element_type=F32).astype(BF16)
            sx[g, :, :, cols] = got.reshape(NX, 16, chunk)
            grads = zc[p, :, :, cols].reshape(2 * tok_dev, chunk)
            got = (weight_col * jnp.dot(pick, grads, preferred_element_type=F32)).astype(BF16)
            sg[p, :, :, cols] = got.reshape(NX, 16, chunk)
            return carry

        lax.fori_loop(0, chunks, body, 0)

    def select_one(g, b):
        index_col, weight_col = columns_of(zm[pairs, b, pl.ds(z, 1), :])
        pick = one_hot(index_col, tok_dev)
        is_grad = jnp.broadcast_to(upper, (64, chunk)) > 0.0

        def body(n, carry):
            cols = pl.ds(pl.multiple_of(n * chunk, chunk), chunk)
            rows = jnp.dot(pick, zx[pairs, b, :, cols], preferred_element_type=F32)
            grads = weight_col * jnp.dot(pick, zc[pairs, b, :, cols], preferred_element_type=F32)
            sx[g, :, :, cols] = jnp.where(is_grad, grads, rows).astype(BF16).reshape(NX, 16, chunk)
            return carry

        lax.fori_loop(0, chunks, body, 0)

    xcp = {}
    x_far, x_next, x_prev = (x + 2) % NX, (x + 1) % NX, (x + 3) % NX
    left_half, right_half = pl.ds(0, dim // 2), pl.ds(dim // 2, dim // 2)

    def x_copy(i, g, src, dst, way):
        xcp[i, g] = send(src, dst, xs_sem.at[i, g], xr_sem.at[i, g], at_x(way))

    def x_stay(i, g, src, dst):
        xcp[i, g] = pltpu.make_async_copy(src, dst, xl_sem.at[i - 8, g])
        xcp[i, g].start()

    def is_pair(g):
        return 1 <= g <= pairs

    def x_send(g):
        if is_pair(g):
            x_copy(0, g, sx.at[g, x_far], lx.at[g], 1)
            x_copy(1, g, sg.at[g - 1, x_far], lg.at[g - 1], -1)
        else:
            x_copy(0, g, sx.at[g, x_far, :, left_half], lx.at[g, :, left_half], 1)
            x_copy(1, g, sx.at[g, x_far, :, right_half], lx.at[g, :, right_half], -1)
        x_copy(2, g, sx.at[g, x_next], rx.at[g, 0, 1], 1)
        x_copy(3, g, sx.at[g, x_prev], rx.at[g, 0, 3], -1)
        x_stay(8, g, sx.at[g, x], rx.at[g, 0, 0])
        if is_pair(g):
            x_copy(4, g, sg.at[g - 1, x_next], rg.at[g - 1, 0, 1], 1)
            x_copy(5, g, sg.at[g - 1, x_prev], rg.at[g - 1, 0, 3], -1)
            x_stay(9, g, sg.at[g - 1, x], rg.at[g - 1, 0, 0])

    def x_relay(g):
        xcp[0, g].wait_recv()
        if is_pair(g):
            x_copy(6, g, lx.at[g], rx.at[g, 0, 2], 1)
        else:
            x_copy(6, g, lx.at[g, :, left_half], rx.at[g, 0, 2, :, left_half], 1)
        xcp[1, g].wait_recv()
        if is_pair(g):
            x_copy(7, g, lg.at[g - 1], rg.at[g - 1, 0, 2], -1)
        else:
            x_copy(7, g, lx.at[g, :, right_half], rx.at[g, 0, 2, :, right_half], -1)

    pcp = {}

    def to_partner(g):
        xcp[8, g].wait()
        for i in (2, 3, 6) if is_pair(g) else (2, 3, 6, 7):
            xcp[i, g].wait_recv()
        pcp[0, g] = send(rx.at[g, 0], rx.at[g, 1], ps_sem.at[0, g], pr_sem.at[0, g], partner)
        if is_pair(g):
            xcp[9, g].wait()
            for i in (4, 5, 7):
                xcp[i, g].wait_recv()
            pcp[1, g] = send(rg.at[g - 1, 0], rg.at[g - 1, 1], ps_sem.at[1, g], pr_sem.at[1, g], partner)

    def arrived(g, n):
        for i in range(g, g + n):
            pcp[0, i].wait_recv()
            if is_pair(i):
                pcp[1, i].wait_recv()

    def times(lhs, rows):
        return lax.dot_general(lhs, rows, (((1,), (1,)), ((), ())), preferred_element_type=F32)

    def pointwise(g, at, width, single, qa, qb):
        def body(i, carry):
            q = qa + i // 2
            rows = pl.ds(pl.multiple_of((i % 2) * (hs // 2), hs // 2), hs // 2)
            pre_gate, pre_up, tan_gate, tan_up, back = [proj[q, k, rows, pl.ds(at, width)] for k in range(5)]
            if single:
                back = pltpu.roll(back, width - CAP, 1)
                is_row = (lax.broadcasted_iota(jnp.int32, (hs // 2, width), 1) // CAP) % 2 == 0
                back = jnp.where(is_row, back, 0.0)
            sig = 1.0 / (1.0 + jnp.exp(-pre_gate))
            first = sig * (1.0 + pre_gate * (1.0 - sig))
            second = sig * (1.0 - sig) * (2.0 + pre_gate * (1.0 - 2.0 * sig))
            cols = pl.ds(g * rows_of, width)
            dirs[q, 0, rows, cols] = (back * (tan_up * first + pre_up * second * tan_gate)).astype(BF16)
            dirs[q, 1, rows, cols] = (back * first * tan_gate).astype(BF16)
            return carry

        lax.fori_loop(0, 2 * (qb - qa), body, 0)

    def terms(g, n, qa, qb):
        width = n * rows_of
        slices = qb - qa

        def body(q, carry):
            got = times(wbuf[q, :4].reshape(4 * hs, dim), rx[g : g + n].reshape(width, dim))
            proj[q, :4, :, pl.ds(0, width)] = got.reshape(4, hs, width)
            return carry

        lax.fori_loop(qa, qb, body, 0)
        down = wbuf[qa:qb, 4].reshape(slices * hs, dim)
        singles = 0 if is_pair(g) else rows_of
        if singles:
            got = times(down, rx[g].reshape(rows_of, dim))
            proj[qa:qb, 4, :, pl.ds(0, rows_of)] = got.reshape(slices, hs, rows_of)
            pointwise(g, 0, rows_of, True, qa, qb)
            g = g + 1
        rest = width - singles
        if rest:
            got = times(down, rg[g - 1 : g - 1 + rest // rows_of].reshape(rest, dim))
            proj[qa:qb, 4, :, pl.ds(singles, rest)] = got.reshape(slices, hs, rest)
            pointwise(g, singles, rest, False, qa, qb)

    def early_product(first, count):
        depth = count * rows_of

        def body(i, carry):
            q = (i // chunks) * 2
            cols = pl.ds(pl.multiple_of((i % chunks) * chunk, chunk), chunk)
            rows = rx[first : first + count, :, :, :, cols].reshape(depth, chunk)
            d = dirs[pl.ds(q, 2), :, :, pl.ds(first * rows_of, depth)].reshape(4 * hs, depth)
            part[pl.ds(q, 2), :, :, cols] = jnp.dot(d, rows, preferred_element_type=F32).reshape(2, 2, hs, chunk)
            return carry

        lax.fori_loop(0, 2 * chunks, body, 0)

    def last_product(q, first, count):
        depth = count * rows_of

        def body(n, carry):
            cols = pl.ds(pl.multiple_of(n * chunk, chunk), chunk)
            rows = rx[first : first + count, :, :, :, cols].reshape(depth, chunk)
            d = dirs[q, :, :, pl.ds(first * rows_of, depth)].reshape(2 * hs, depth)
            acc = part[q, :, :, cols] + jnp.dot(d, rows, preferred_element_type=F32).reshape(2, hs, chunk)
            gate, up = acc[0], acc[1]
            if q == QFAR:
                sb[0, :, cols] = gate.astype(BF16)
                sb[1, :, cols] = up.astype(BF16)
            elif q == QNEXT:
                part[q, 0, :, cols] = gate
                sb[2, :, cols] = up.astype(BF16)
            elif q == QPREV:
                sb[3, :, cols] = gate.astype(BF16)
                part[q, 1, :, cols] = up
            else:
                out_ref[0, 0, :, cols] = gate
                out_ref[0, 1, :, cols] = up
            return carry

        lax.fori_loop(0, chunks, body, 0)

    rcp = {}

    def r_send(i, src, way, cols=slice(None)):
        rcp[i] = send(sb.at[src, :, cols], rb.at[src, :, cols], rs_sem.at[i], rr_sem.at[i], at_y(way))

    def z_step(s):
        for way, kind in z_lanes(s):
            zcp[way, kind, s].wait_recv()
            if s < steps and (way, kind) in z_lanes(s + 1):
                zcp[way, kind, s + 1] = z_send(way, kind, s + 1)

    local[0].wait()
    local[1].wait()
    select_one(own, 0)
    x_send(own)
    for s in range(1, steps):
        z_step(s)
        select(s)
        x_send(s)
        x_relay(s - 1)
        if s >= 2:
            to_partner(s - 2)
        if s == 3:
            y_forward()
        if s == steps - 2:
            y_near()
            arrived(own, 2)
            terms(own, 2, QNEXT, 4)
        if s == steps - 1:
            arrived(2, 2)
            terms(2, 2, QNEXT, 4)
    x_relay(pairs)
    y_finish()
    terms(own, 2, QFAR, QNEXT)
    terms(2, 2, QFAR, QNEXT)
    z_step(steps)
    select_one(far, 1)
    x_send(far)
    to_partner(pairs - 1)
    arrived(4, 2)
    terms(4, 2, 0, 4)
    x_relay(far)
    to_partner(pairs)
    early_product(0, 6)
    to_partner(far)
    arrived(6, 2)
    terms(6, 2, 0, 4)
    arrived(far, 1)
    terms(far, 1, QFAR, QNEXT)
    last_product(QFAR, 6, 3)
    r_send(0, 0, 1)
    r_send(1, 1, -1)
    terms(far, 1, QNEXT, 4)
    last_product(QNEXT, 6, 3)
    r_send(2, 2, 1)
    last_product(QPREV, 6, 3)
    r_send(3, 3, -1)
    last_product(QOWN, 6, 3)
    rcp[0].wait_recv()
    sb[4] = (part[QNEXT, 0] + rb[0].astype(F32)).astype(BF16)
    r_send(4, 4, 1, left_half)
    r_send(5, 4, 1, right_half)
    rcp[1].wait_recv()
    sb[5] = (part[QPREV, 1] + rb[1].astype(F32)).astype(BF16)
    r_send(6, 5, -1, left_half)
    r_send(7, 5, -1, right_half)
    rcp[2].wait_recv()
    out_ref[0, 1] += rb[2].astype(F32)
    rcp[3].wait_recv()
    out_ref[0, 0] += rb[3].astype(F32)
    for i, cols in ((4, left_half), (6, left_half), (5, right_half), (7, right_half)):
        rcp[i].wait_recv()
        which = 0 if i < 6 else 1
        out_ref[0, which, :, cols] += rb[4 + which, :, cols].astype(F32)
    for c in sent:
        c.wait_send()


def local(tokens, cotangent, routes, combine, w_in, w_out, v_in):
    nz = lax.axis_size("expert") // NX
    pairs = nz // 2 - 1
    groups = pairs + 2
    tok_dev, dim = tokens.shape
    hs = w_out.shape[1]
    rows_of = 2 * NX * 16
    any_spec = pl.BlockSpec(memory_space=pl.ANY)
    vmem_spec = pl.BlockSpec(memory_space=pltpu.VMEM)
    dma = pltpu.SemaphoreType.DMA
    return pl.pallas_call(
        functools.partial(kernel, nz),
        out_shape=jax.ShapeDtypeStruct((1, 2, hs, dim), F32),
        in_specs=[any_spec, any_spec, vmem_spec, vmem_spec, any_spec, any_spec, any_spec],
        out_specs=vmem_spec,
        scratch_shapes=[
            pltpu.VMEM((pairs + 1, 2, tok_dev, dim), BF16),
            pltpu.VMEM((pairs + 1, 2, tok_dev, dim), BF16),
            pltpu.VMEM((pairs + 1, 2, nz, 128), F32),
            pltpu.VMEM((groups, NX, 16, dim), BF16),
            pltpu.VMEM((pairs, NX, 16, dim), BF16),
            pltpu.VMEM((groups, 16, dim), BF16),
            pltpu.VMEM((pairs, 16, dim), BF16),
            pltpu.VMEM((groups, 2, NX, 16, dim), BF16),
            pltpu.VMEM((pairs, 2, NX, 16, dim), BF16),
            pltpu.VMEM((4, 5, hs, dim), BF16),
            pltpu.VMEM((4, 5, hs, 2 * rows_of), F32),
            pltpu.VMEM((4, 2, hs, groups * rows_of), BF16),
            pltpu.VMEM((4, 2, hs, dim), F32),
            pltpu.VMEM((6, hs, dim), BF16),
            pltpu.VMEM((6, hs, dim), BF16),
            dma((5,)),
            dma((2, 3, pairs + 1)),
            dma((2, 3, pairs + 1)),
            dma((2, 6)),
            dma((2, 6)),
            dma((8, groups)),
            dma((8, groups)),
            dma((2, groups)),
            dma((2, groups)),
            dma((2, groups)),
            dma((8,)),
            dma((8,)),
        ],
        compiler_params=pltpu.CompilerParams(
            collective_id=0, has_side_effects=True, vmem_limit_bytes=60 * 1024 * 1024
        ),
    )(tokens, cotangent, routes.T, combine.T, w_in, w_out, v_in)


def solution(mesh):
    in_specs = (
        P(("dp", "expert"), None),
        P(("dp", "expert"), None),
        P(("dp", "expert"), None),
        P(("dp", "expert"), None),
        P("expert", None, "dp", None),
        P("expert", "dp", None),
        P("expert", None, "dp", None),
    )
    out_specs = P("expert", None, "dp", None)
    return jax.shard_map(local, mesh=mesh, in_specs=in_specs, out_specs=out_specs, check_vma=False)
```

```python
import functools

import jax
import jax.numpy as jnp
from jax import lax
from jax.experimental import pallas as pl
from jax.experimental.pallas import tpu as pltpu
from jax.sharding import PartitionSpec as P

MESH = pl.DeviceIdType.MESH
F32 = jnp.float32
BF16 = jnp.bfloat16
NX = 4
NY = 4
NC = 2
CAP = 8
QFAR, QNEXT, QPREV, QOWN = 0, 1, 2, 3


def kernel(
    nz, tok_hbm, cot_hbm, routes_hbm, combine_hbm, win_hbm, wout_hbm, vin_hbm, mine_hbm, theirs_hbm,
    routes_ref, combine_ref, zx, zc, zm, sx, sg, lx, lg, rx, rg, wbuf, proj, dirs, part, sb, rb,
    loc_sem, zs_sem, zr_sem, ys_sem, yr_sem, xs_sem, xr_sem, xl_sem, ps_sem, pr_sem, rs_sem, rr_sem,
):
    steps = nz // 2
    pairs = steps - 1
    own, far = 0, pairs + 1
    tok_dev, dim = tok_hbm.shape
    top = routes_hbm.shape[0]
    hs = wout_hbm.shape[1]
    rows_of = 2 * NX * 16
    dp = lax.axis_index("dp")
    ex = lax.axis_index("expert")
    y, core = dp // NC, dp % NC
    x, z = ex // nz, ex % nz

    def at_z(k):
        return (dp, x * nz + (z + k + nz) % nz)

    def at_x(k):
        return (dp, ((x + k + NX) % NX) * nz + z)

    def at_y(k):
        return (((y + k + NY) % NY) * NC + core, ex)

    partner = (y * NC + (1 - core), ex)

    barrier = pltpu.get_barrier_semaphore()
    neighbours = [at_z(1), at_z(-1), at_x(1), at_x(-1), at_y(1), at_y(-1), partner]
    for n in neighbours:
        pl.semaphore_signal(barrier, inc=1, device_id=n, device_id_type=MESH)

    named = [
        pltpu.make_async_copy(routes_hbm, routes_ref, loc_sem.at[5]),
        pltpu.make_async_copy(combine_hbm, combine_ref, loc_sem.at[6]),
    ]
    local = [
        pltpu.make_async_copy(tok_hbm, zx.at[pairs, 0], loc_sem.at[0]),
        pltpu.make_async_copy(cot_hbm, zc.at[pairs, 0], loc_sem.at[1]),
        pltpu.make_async_copy(win_hbm.at[0], wbuf.at[QOWN, pl.ds(0, 2)], loc_sem.at[2]),
        pltpu.make_async_copy(vin_hbm.at[0], wbuf.at[QOWN, pl.ds(2, 2)], loc_sem.at[3]),
        pltpu.make_async_copy(wout_hbm.at[0], wbuf.at[QOWN, 4], loc_sem.at[4]),
    ]
    for c in named + local:
        c.start()
    pl.semaphore_wait(barrier, len(neighbours))

    sent = []

    def send(src, dst, ssem, rsem, device):
        c = pltpu.make_async_remote_copy(
            src_ref=src, dst_ref=dst, send_sem=ssem, recv_sem=rsem, device_id=device, device_id_type=MESH
        )
        c.start()
        sent.append(c)
        return c

    left_half, right_half = pl.ds(0, dim // 2), pl.ds(dim // 2, dim // 2)
    zbuf = (zx, zc, zm)

    def z_send(way, kind, s):
        part_of = slice(None)
        buf = zbuf[way if kind == 3 else kind]
        if s == steps and kind != 2:
            part_of = right_half if kind == 3 else left_half
        dst = (s - 1, way) if s < steps else (pairs, 1)
        if s > 1:
            src = buf.at[s - 2, way, :, part_of]
        elif kind == 2:
            src = buf.at[pairs, 0]
        else:
            src = (tok_hbm, cot_hbm)[kind]
        return send(
            src, buf.at[dst[0], dst[1], :, part_of], zs_sem.at[way, kind, s - 1], zr_sem.at[way, kind, s - 1],
            at_z(1 if way == 0 else -1),
        )

    tables, tokens, cotangents = [(0, 2), (1, 2)], [(0, 0), (1, 0)], [(0, 1), (1, 1)]
    far_lanes = [(0, 2)], [(0, 0), (1, 1)], [(0, 3), (1, 3)]
    zcp = {}

    def z_start(lanes, s):
        for way, kind in lanes:
            zcp[way, kind, s] = z_send(way, kind, s)

    def z_wait(lanes, s):
        for way, kind in lanes:
            zcp[way, kind, s].wait_recv()
            if s < steps - 1:
                z_start([(way, kind)], s + 1)
            elif s == steps - 1:
                if (way, kind) in ((0, 0), (1, 1)):
                    z_start([(way, kind), (way, 3)], s + 1)
                elif (way, kind) == (0, 2):
                    z_start([(way, kind)], s + 1)

    z_start(tokens, 1)

    half_rows = hs // 2

    def piece(q, i):
        if i == 0:
            return wbuf.at[q, pl.ds(0, 2)]
        if i == 1:
            return wbuf.at[q, 4, pl.ds(0, half_rows)]
        if i == 2:
            return wbuf.at[q, pl.ds(2, 2)]
        return wbuf.at[q, 4, pl.ds(half_rows, half_rows)]

    own_piece = (
        win_hbm.at[0], wout_hbm.at[0, pl.ds(0, half_rows)], vin_hbm.at[0], wout_hbm.at[0, pl.ds(half_rows, half_rows)]
    )
    ycp = {}
    for n in range(4):
        for way in (0, 1):
            i = n if way == 0 else (n + 2) % 4
            ycp[way, i] = send(
                own_piece[i], piece(QPREV if way == 0 else QNEXT, i),
                ys_sem.at[way, i], yr_sem.at[way, i], at_y(1 if way == 0 else -1),
            )

    def y_forward():
        for n in range(2):
            for way in (0, 1):
                i = n if way == 0 else n + 2
                ycp[way, i].wait_recv()
                ycp[way, 4 + n] = send(
                    piece(QPREV if way == 0 else QNEXT, i), piece(QFAR, i),
                    ys_sem.at[way, 4 + n], yr_sem.at[way, 4 + n], at_y(1 if way == 0 else -1),
                )

    def y_near():
        for c in local[2:]:
            c.wait()
        for way in (0, 1):
            for n in range(2):
                ycp[way, (n + 2) % 4 if way == 0 else n].wait_recv()

    def y_finish():
        for way in (0, 1):
            for n in range(2):
                ycp[way, 4 + n].wait_recv()

    lane = lax.broadcasted_iota(jnp.int32, (tok_dev, 128), 1)
    token_i = lax.broadcasted_iota(jnp.int32, (tok_dev, tok_dev), 0)
    token_j = lax.broadcasted_iota(jnp.int32, (tok_dev, tok_dev), 1)
    token_f = lax.broadcasted_iota(jnp.int32, (tok_dev, 128), 0).astype(F32)
    slot_f = (lane % CAP).astype(F32)
    expert_x = ((lane % 64) // 16) * nz
    earlier = jnp.where(token_j < token_i, 1.0, 0.0).astype(BF16)

    def column(row):
        picked = jnp.where(token_i == token_j, jnp.broadcast_to(row, (tok_dev, tok_dev)), 0.0)
        return jnp.broadcast_to(jnp.sum(picked, axis=1, keepdims=True), (tok_dev, 128))

    for c in named:
        c.wait()
    routes = [column(routes_ref[k : k + 1, :].astype(F32)) for k in range(top)]
    combine = [column(combine_ref[k : k + 1, :]) for k in range(top)]

    def table_row(zz):
        wanted = (expert_x + zz).astype(F32)
        member = jnp.zeros((tok_dev, 128), F32)
        weight = jnp.zeros((tok_dev, 128), F32)
        for k in range(top):
            hit = routes[k] == wanted
            member = jnp.where(hit, 1.0, member)
            weight = jnp.where(hit, combine[k], weight)
        rank = jnp.dot(earlier, member.astype(BF16), preferred_element_type=F32)
        chosen = jnp.where(rank == slot_f, member, 0.0)
        value = jnp.where(lane < 64, token_f + 1.0, weight)
        total = jnp.sum(chosen * value, axis=0, keepdims=True)
        zm[pairs, 0, pl.ds(zz, 1), :] = jnp.where(lane[:1] < 64, total - 1.0, total)

    def table_rows(i, carry):
        for j in range(4):
            table_row(i * 4 + j)
        return carry

    lax.fori_loop(0, nz // 4, table_rows, 0)

    z_start(tables + cotangents, 1)

    srow = lax.broadcasted_iota(jnp.int32, (64, 128), 0)
    slane = lax.broadcasted_iota(jnp.int32, (64, 128), 1)
    upper = ((srow[:, :1] // 8) % 2).astype(F32)
    chunk = min(512, dim)
    chunks = dim // chunk

    def columns_of(m):
        m = jnp.broadcast_to(m, (64, 128))
        index_col = jnp.sum(jnp.where(slane == srow, m, 0.0), axis=1, keepdims=True)
        weight_col = jnp.sum(jnp.where(slane == srow + 64, m, 0.0), axis=1, keepdims=True)
        return index_col, weight_col

    def one_hot(index_col, width):
        tokens = lax.broadcasted_iota(jnp.int32, (64, width), 1).astype(F32)
        return jnp.where(index_col == tokens, 1.0, 0.0).astype(BF16)

    def pick_of(g):
        p = g - 1
        ma = zm[p, 0, pl.ds(z, 1), :]
        mb = zm[p, 1, pl.ds(z, 1), :]
        index_col, weight_col = columns_of(jnp.where((slane[:1] // 8) % 2 == 0, ma, mb))
        index_col = jnp.where(index_col >= 0.0, index_col + upper * tok_dev, -1.0)
        return one_hot(index_col, 2 * tok_dev), weight_col

    def select_rows(g, pick):
        def body(n, carry):
            cols = pl.ds(pl.multiple_of(n * chunk, chunk), chunk)
            rows = zx[g - 1, :, :, cols].reshape(2 * tok_dev, chunk)
            got = jnp.dot(pick, rows, preferred_element_type=F32).astype(BF16)
            sx[g, :, :, cols] = got.reshape(NX, 16, chunk)
            return carry

        lax.fori_loop(0, chunks, body, 0)

    def select_grads(g, pick, weight_col):
        def body(n, carry):
            cols = pl.ds(pl.multiple_of(n * chunk, chunk), chunk)
            grads = zc[g - 1, :, :, cols].reshape(2 * tok_dev, chunk)
            got = (weight_col * jnp.dot(pick, grads, preferred_element_type=F32)).astype(BF16)
            sg[g - 1, :, :, cols] = got.reshape(NX, 16, chunk)
            return carry

        lax.fori_loop(0, chunks, body, 0)

    def select_one(g, b, first, count):
        index_col, weight_col = columns_of(zm[pairs, b, pl.ds(z, 1), :])
        pick = one_hot(index_col, tok_dev)
        is_grad = jnp.broadcast_to(upper, (64, chunk)) > 0.0

        def body(n, carry):
            cols = pl.ds(pl.multiple_of(n * chunk, chunk), chunk)
            rows = jnp.dot(pick, zx[pairs, b, :, cols], preferred_element_type=F32)
            grads = weight_col * jnp.dot(pick, zc[pairs, b, :, cols], preferred_element_type=F32)
            sx[g, :, :, cols] = jnp.where(is_grad, grads, rows).astype(BF16).reshape(NX, 16, chunk)
            return carry

        lax.fori_loop(first, first + count, body, 0)

    xcp = {}
    x_far, x_next, x_prev = (x + 2) % NX, (x + 1) % NX, (x + 3) % NX

    def x_copy(i, g, src, dst, way):
        xcp[i, g] = send(src, dst, xs_sem.at[i, g], xr_sem.at[i, g], at_x(way))

    def x_stay(i, g, src, dst):
        xcp[i, g] = pltpu.make_async_copy(src, dst, xl_sem.at[i - 8, g])
        xcp[i, g].start()

    def is_pair(g):
        return 1 <= g <= pairs

    def send_rows(g):
        x_copy(0, g, sx.at[g, x_far], lx.at[g], 1)
        x_copy(2, g, sx.at[g, x_next], rx.at[g, 0, 1], 1)
        x_copy(3, g, sx.at[g, x_prev], rx.at[g, 0, 3], -1)
        x_stay(8, g, sx.at[g, x], rx.at[g, 0, 0])

    def send_grads(g):
        x_copy(1, g, sg.at[g - 1, x_far], lg.at[g - 1], -1)
        x_copy(5, g, sg.at[g - 1, x_prev], rg.at[g - 1, 0, 3], -1)
        x_copy(4, g, sg.at[g - 1, x_next], rg.at[g - 1, 0, 1], 1)
        x_stay(9, g, sg.at[g - 1, x], rg.at[g - 1, 0, 0])

    def send_left(g):
        x_copy(0, g, sx.at[g, x_far, :, left_half], lx.at[g, :, left_half], 1)
        x_copy(2, g, sx.at[g, x_next, :, left_half], rx.at[g, 0, 1, :, left_half], 1)
        x_copy(3, g, sx.at[g, x_prev, :, left_half], rx.at[g, 0, 3, :, left_half], -1)
        x_stay(8, g, sx.at[g, x, :, left_half], rx.at[g, 0, 0, :, left_half])

    def send_right(g):
        x_copy(1, g, sx.at[g, x_far, :, right_half], lx.at[g, :, right_half], -1)
        x_copy(5, g, sx.at[g, x_prev, :, right_half], rx.at[g, 0, 3, :, right_half], -1)
        x_copy(4, g, sx.at[g, x_next, :, right_half], rx.at[g, 0, 1, :, right_half], 1)
        x_stay(9, g, sx.at[g, x, :, right_half], rx.at[g, 0, 0, :, right_half])

    def is_pair(g):
        return 1 <= g <= pairs

    def relay_first(g):
        xcp[0, g].wait_recv()
        if is_pair(g):
            x_copy(6, g, lx.at[g], rx.at[g, 0, 2], 1)
        else:
            x_copy(6, g, lx.at[g, :, left_half], rx.at[g, 0, 2, :, left_half], 1)

    def relay_second(g):
        xcp[1, g].wait_recv()
        if is_pair(g):
            x_copy(7, g, lg.at[g - 1], rg.at[g - 1, 0, 2], -1)
        else:
            x_copy(7, g, lx.at[g, :, right_half], rx.at[g, 0, 2, :, right_half], -1)

    pcp = {}

    def share(i, g, buf, h, cols=slice(None)):
        pcp[i, g] = send(
            buf.at[h, 0, :, :, cols], buf.at[h, 1, :, :, cols], ps_sem.at[i, g], pr_sem.at[i, g], partner
        )

    def share_first(g):
        xcp[8, g].wait()
        for i in (2, 3, 6):
            xcp[i, g].wait_recv()
        if is_pair(g):
            share(0, g, rx, g)
        else:
            share(0, g, rx, g, left_half)

    def share_second(g):
        xcp[9, g].wait()
        for i in (4, 5, 7):
            xcp[i, g].wait_recv()
        if is_pair(g):
            share(1, g, rg, g - 1)
        else:
            share(1, g, rx, g, right_half)

    def arrived(g, n):
        for i in range(g, g + n):
            pcp[0, i].wait_recv()
            pcp[1, i].wait_recv()

    def times(lhs, rows):
        return lax.dot_general(lhs, rows, (((1,), (1,)), ((), ())), preferred_element_type=F32)

    def pointwise(g, at, width, single, qa, qb):
        def body(i, carry):
            q = qa + i // 2
            rows = pl.ds(pl.multiple_of((i % 2) * (hs // 2), hs // 2), hs // 2)
            pre_gate, pre_up, tan_gate, tan_up, back = [proj[q, k, rows, pl.ds(at, width)] for k in range(5)]
            if single:
                back = pltpu.roll(back, width - CAP, 1)
                is_row = (lax.broadcasted_iota(jnp.int32, (hs // 2, width), 1) // CAP) % 2 == 0
                back = jnp.where(is_row, back, 0.0)
            sig = 1.0 / (1.0 + jnp.exp(-pre_gate))
            first = sig * (1.0 + pre_gate * (1.0 - sig))
            second = sig * (1.0 - sig) * (2.0 + pre_gate * (1.0 - 2.0 * sig))
            cols = pl.ds(g * rows_of, width)
            dirs[q, 0, rows, cols] = (back * (tan_up * first + pre_up * second * tan_gate)).astype(BF16)
            dirs[q, 1, rows, cols] = (back * first * tan_gate).astype(BF16)
            return carry

        lax.fori_loop(0, 2 * (qb - qa), body, 0)

    def terms(g, n, qa, qb):
        width = n * rows_of
        slices = qb - qa

        got = times(wbuf[qa:qb, :4].reshape(slices * 4 * hs, dim), rx[g : g + n].reshape(width, dim))
        proj[qa:qb, :4, :, pl.ds(0, width)] = got.reshape(slices, 4, hs, width)
        down = wbuf[qa:qb, 4].reshape(slices * hs, dim)
        singles = 0 if is_pair(g) else rows_of
        if singles:
            got = times(down, rx[g].reshape(rows_of, dim))
            proj[qa:qb, 4, :, pl.ds(0, rows_of)] = got.reshape(slices, hs, rows_of)
            pointwise(g, 0, rows_of, True, qa, qb)
            g = g + 1
        rest = width - singles
        if rest:
            got = times(down, rg[g - 1 : g - 1 + rest // rows_of].reshape(rest, dim))
            proj[qa:qb, 4, :, pl.ds(singles, rest)] = got.reshape(slices, hs, rest)
            pointwise(g, singles, rest, False, qa, qb)

    def early_product(qa, qb, first, count, add):
        depth = count * rows_of
        slices = qb - qa
        wide = chunk if slices == 1 else chunk // 2

        def body(i, carry):
            cols = pl.ds(pl.multiple_of(i * wide, wide), wide)
            rows = rx[first : first + count, :, :, :, cols].reshape(depth, wide)
            d = dirs[qa:qb, :, :, pl.ds(first * rows_of, depth)].reshape(slices * 2 * hs, depth)
            value = jnp.dot(d, rows, preferred_element_type=F32).reshape(slices, 2, hs, wide)
            part[qa:qb, :, :, cols] = part[qa:qb, :, :, cols] + value if add else value
            return carry

        lax.fori_loop(0, dim // wide, body, 0)

    def last_product(q, first, count):
        depth = count * rows_of

        def body(n, carry):
            cols = pl.ds(pl.multiple_of(n * chunk, chunk), chunk)
            rows = rx[first : first + count, :, :, :, cols].reshape(depth, chunk)
            d = dirs[q, :, :, pl.ds(first * rows_of, depth)].reshape(2 * hs, depth)
            acc = part[q, :, :, cols] + jnp.dot(d, rows, preferred_element_type=F32).reshape(2, hs, chunk)
            gate, up = acc[0], acc[1]
            if q == QFAR:
                sb[0, :, cols] = gate.astype(BF16)
                sb[1, :, cols] = up.astype(BF16)
            elif q == QNEXT:
                part[q, 0, :, cols] = gate
                sb[2, :, cols] = up.astype(BF16)
            elif q == QPREV:
                sb[3, :, cols] = gate.astype(BF16)
                part[q, 1, :, cols] = up
            else:
                part[q, :, :, cols] = acc
            return carry

        lax.fori_loop(0, chunks, body, 0)

    rcp = {}

    def r_send(i, src, dst, way):
        rcp[i] = send(sb.at[src], dst, rs_sem.at[i], rr_sem.at[i], at_y(way))

    local[0].wait()
    local[1].wait()
    select_one(own, 0, 0, chunks)
    send_left(own)
    send_right(own)
    for s in range(1, steps):
        z_wait(tokens + tables, s)
        pick, weight_col = pick_of(s)
        select_rows(s, pick)
        send_rows(s)
        relay_first(s - 1)
        if s >= 2:
            share_first(s - 2)
        if s == steps - 2:
            y_near()
            arrived(own, 2)
            terms(own, 2, QNEXT, 4)
        if s == steps - 1:
            early_product(QNEXT, 4, own, 4, False)
        z_wait(cotangents, s)
        select_grads(s, pick, weight_col)
        send_grads(s)
        relay_second(s - 1)
        if s >= 2:
            share_second(s - 2)
        if s == 3:
            y_forward()
        if s == steps - 2:
            arrived(2, 2)
            terms(2, 2, QNEXT, 4)
    arrived(4, 2)
    terms(4, 2, QNEXT, 4)
    z_wait(far_lanes[1] + far_lanes[0], steps)
    select_one(far, 1, 0, chunks // 2)
    send_left(far)
    relay_first(pairs)
    share_first(pairs - 1)
    z_wait(far_lanes[2], steps)
    select_one(far, 1, chunks // 2, chunks // 2)
    send_right(far)
    relay_second(pairs)
    share_second(pairs - 1)
    y_finish()
    for g in (own, 2, 4):
        terms(g, 2, QFAR, QNEXT)
    relay_first(far)
    relay_second(far)
    share_first(pairs)
    share_second(pairs)
    early_product(QFAR, QNEXT, own, 6, False)
    early_product(QNEXT, 4, 4, 2, True)
    arrived(6, 2)
    terms(6, 2, QFAR, QNEXT)
    share_first(far)
    share_second(far)
    terms(6, 2, QNEXT, QPREV)
    arrived(far, 1)
    terms(far, 1, QFAR, QNEXT)
    last_product(QFAR, 6, 3)
    r_send(0, 0, rb.at[0], 1)
    r_send(1, 1, rb.at[1], -1)
    terms(6, 2, QPREV, 4)
    terms(far, 1, QNEXT, 4)
    last_product(QNEXT, 6, 3)
    r_send(2, 2, theirs_hbm.at[0, 0, 1], 1)
    last_product(QPREV, 6, 3)
    r_send(3, 3, theirs_hbm.at[1, 0, 0], -1)
    last_product(QOWN, 6, 3)
    keep = pltpu.make_async_copy(part.at[QOWN], mine_hbm.at[0], loc_sem.at[0])
    keep.start()
    rcp[0].wait_recv()
    sb[4] = (part[QNEXT, 0] + rb[0].astype(F32)).astype(BF16)
    r_send(4, 4, theirs_hbm.at[0, 0, 0], 1)
    rcp[1].wait_recv()
    sb[5] = (part[QPREV, 1] + rb[1].astype(F32)).astype(BF16)
    r_send(5, 5, theirs_hbm.at[1, 0, 1], -1)
    keep.wait()
    for i in range(2, 6):
        rcp[i].wait_recv()
    for c in sent:
        c.wait_send()


def local(tokens, cotangent, routes, combine, w_in, w_out, v_in):
    nz = lax.axis_size("expert") // NX
    pairs = nz // 2 - 1
    groups = pairs + 2
    tok_dev, dim = tokens.shape
    hs = w_out.shape[1]
    top = routes.shape[1]
    rows_of = 2 * NX * 16
    any_spec = pl.BlockSpec(memory_space=pl.ANY)
    dma = pltpu.SemaphoreType.DMA
    mine, theirs = pl.pallas_call(
        functools.partial(kernel, nz),
        out_shape=(
            jax.ShapeDtypeStruct((1, 2, hs, dim), F32),
            jax.ShapeDtypeStruct((2, 1, 2, hs, dim), BF16),
        ),
        in_specs=[any_spec] * 7,
        out_specs=(any_spec, any_spec),
        scratch_shapes=[
            pltpu.VMEM((top, tok_dev), jnp.int32),
            pltpu.VMEM((top, tok_dev), F32),
            pltpu.VMEM((pairs + 1, 2, tok_dev, dim), BF16),
            pltpu.VMEM((pairs + 1, 2, tok_dev, dim), BF16),
            pltpu.VMEM((pairs + 1, 2, nz, 128), F32),
            pltpu.VMEM((groups, NX, 16, dim), BF16),
            pltpu.VMEM((pairs, NX, 16, dim), BF16),
            pltpu.VMEM((groups, 16, dim), BF16),
            pltpu.VMEM((pairs, 16, dim), BF16),
            pltpu.VMEM((groups, 2, NX, 16, dim), BF16),
            pltpu.VMEM((pairs, 2, NX, 16, dim), BF16),
            pltpu.VMEM((4, 5, hs, dim), BF16),
            pltpu.VMEM((4, 5, hs, 2 * rows_of), F32),
            pltpu.VMEM((4, 2, hs, groups * rows_of), BF16),
            pltpu.VMEM((4, 2, hs, dim), F32),
            pltpu.VMEM((6, hs, dim), BF16),
            pltpu.VMEM((2, hs, dim), BF16),
            dma((7,)),
            dma((2, 4, pairs + 1)),
            dma((2, 4, pairs + 1)),
            dma((2, 6)),
            dma((2, 6)),
            dma((8, groups)),
            dma((8, groups)),
            dma((2, groups)),
            dma((2, groups)),
            dma((2, groups)),
            dma((6,)),
            dma((6,)),
        ],
        compiler_params=pltpu.CompilerParams(
            collective_id=0, has_side_effects=True, vmem_limit_bytes=60 * 1024 * 1024
        ),
    )(tokens, cotangent, routes.T, combine.T, w_in, w_out, v_in)
    return mine + theirs[0].astype(F32) + theirs[1].astype(F32)


def solution(mesh):
    in_specs = (
        P(("dp", "expert"), None),
        P(("dp", "expert"), None),
        P(("dp", "expert"), None),
        P(("dp", "expert"), None),
        P("expert", None, "dp", None),
        P("expert", "dp", None),
        P("expert", None, "dp", None),
    )
    out_specs = P("expert", None, "dp", None)
    return jax.shard_map(local, mesh=mesh, in_specs=in_specs, out_specs=out_specs, check_vma=False)
```

```python
import functools

import jax
import jax.numpy as jnp
from jax import lax
from jax.experimental import pallas as pl
from jax.experimental.pallas import tpu as pltpu
from jax.sharding import PartitionSpec as P

MESH = pl.DeviceIdType.MESH
F32 = jnp.float32
BF16 = jnp.bfloat16
NX = 4
NY = 4
NC = 2
CAP = 8
QFAR, QNEXT, QPREV, QOWN = 0, 1, 2, 3


def kernel(
    nz, tok_hbm, cot_hbm, routes_hbm, combine_hbm, win_hbm, wout_hbm, vin_hbm, mine_hbm, theirs_hbm,
    routes_ref, combine_ref, zx, zc, zm, sx, sg, lx, lg, rx, rg, wbuf, proj, dirs, part, sb, rb,
    loc_sem, zs_sem, zr_sem, ys_sem, yr_sem, xs_sem, xr_sem, xl_sem, ps_sem, pr_sem, rs_sem, rr_sem,
):
    steps = nz // 2
    pairs = steps - 1
    own, far = 0, pairs + 1
    tok_dev, dim = tok_hbm.shape
    top = routes_hbm.shape[0]
    hs = wout_hbm.shape[1]
    rows_of = 2 * NX * 16
    dp = lax.axis_index("dp")
    ex = lax.axis_index("expert")
    y, core = dp // NC, dp % NC
    x, z = ex // nz, ex % nz

    def at_z(k):
        return (dp, x * nz + (z + k + nz) % nz)

    def at_x(k):
        return (dp, ((x + k + NX) % NX) * nz + z)

    def at_y(k):
        return (((y + k + NY) % NY) * NC + core, ex)

    partner = (y * NC + (1 - core), ex)

    barrier = pltpu.get_barrier_semaphore()
    neighbours = [at_z(1), at_z(-1), at_x(1), at_x(-1), at_y(1), at_y(-1), partner]
    for n in neighbours:
        pl.semaphore_signal(barrier, inc=1, device_id=n, device_id_type=MESH)

    named = [
        pltpu.make_async_copy(routes_hbm, routes_ref, loc_sem.at[5]),
        pltpu.make_async_copy(combine_hbm, combine_ref, loc_sem.at[6]),
    ]
    local = [
        pltpu.make_async_copy(tok_hbm, zx.at[pairs, 0], loc_sem.at[0]),
        pltpu.make_async_copy(cot_hbm, zc.at[pairs, 0], loc_sem.at[1]),
        pltpu.make_async_copy(win_hbm.at[0], wbuf.at[QOWN, pl.ds(0, 2)], loc_sem.at[2]),
        pltpu.make_async_copy(vin_hbm.at[0], wbuf.at[QOWN, pl.ds(2, 2)], loc_sem.at[3]),
        pltpu.make_async_copy(wout_hbm.at[0], wbuf.at[QOWN, 4], loc_sem.at[4]),
    ]
    for c in named + local:
        c.start()
    pl.semaphore_wait(barrier, len(neighbours))

    sent = []

    def send(src, dst, ssem, rsem, device):
        c = pltpu.make_async_remote_copy(
            src_ref=src, dst_ref=dst, send_sem=ssem, recv_sem=rsem, device_id=device, device_id_type=MESH
        )
        c.start()
        sent.append(c)
        return c

    left_half, right_half = pl.ds(0, dim // 2), pl.ds(dim // 2, dim // 2)
    zbuf = (zx, zc, zm)

    def z_send(way, kind, s):
        part_of = slice(None)
        buf = zbuf[way if kind == 3 else kind]
        if s == steps and kind != 2:
            part_of = right_half if kind == 3 else left_half
        dst = (s - 1, way) if s < steps else (pairs, 1)
        if s > 1:
            src = buf.at[s - 2, way, :, part_of]
        elif kind == 2:
            src = buf.at[pairs, 0]
        else:
            src = (tok_hbm, cot_hbm)[kind]
        return send(
            src, buf.at[dst[0], dst[1], :, part_of], zs_sem.at[way, kind, s - 1], zr_sem.at[way, kind, s - 1],
            at_z(1 if way == 0 else -1),
        )

    tables, tokens, cotangents = [(0, 2), (1, 2)], [(0, 0), (1, 0)], [(0, 1), (1, 1)]
    far_lanes = [(0, 2)], [(0, 0), (1, 1)], [(0, 3), (1, 3)]
    zcp = {}

    def z_start(lanes, s):
        for way, kind in lanes:
            zcp[way, kind, s] = z_send(way, kind, s)

    def z_wait(lanes, s):
        for way, kind in lanes:
            zcp[way, kind, s].wait_recv()
            if s < steps - 1:
                z_start([(way, kind)], s + 1)
            elif s == steps - 1:
                if (way, kind) in ((0, 0), (1, 1)):
                    z_start([(way, kind), (way, 3)], s + 1)
                elif (way, kind) == (0, 2):
                    z_start([(way, kind)], s + 1)

    z_start(tokens, 1)

    half_rows = hs // 2

    def piece(q, i):
        if i == 0:
            return wbuf.at[q, pl.ds(0, 2)]
        if i == 1:
            return wbuf.at[q, 4, pl.ds(0, half_rows)]
        if i == 2:
            return wbuf.at[q, pl.ds(2, 2)]
        return wbuf.at[q, 4, pl.ds(half_rows, half_rows)]

    own_piece = (
        win_hbm.at[0], wout_hbm.at[0, pl.ds(0, half_rows)], vin_hbm.at[0], wout_hbm.at[0, pl.ds(half_rows, half_rows)]
    )
    ycp = {}
    for n in range(4):
        for way in (0, 1):
            i = n if way == 0 else (n + 2) % 4
            ycp[way, i] = send(
                own_piece[i], piece(QPREV if way == 0 else QNEXT, i),
                ys_sem.at[way, i], yr_sem.at[way, i], at_y(1 if way == 0 else -1),
            )

    def y_forward():
        for n in range(2):
            for way in (0, 1):
                i = n if way == 0 else n + 2
                ycp[way, i].wait_recv()
                ycp[way, 4 + n] = send(
                    piece(QPREV if way == 0 else QNEXT, i), piece(QFAR, i),
                    ys_sem.at[way, 4 + n], yr_sem.at[way, 4 + n], at_y(1 if way == 0 else -1),
                )

    def y_near():
        for c in local[2:]:
            c.wait()
        for way in (0, 1):
            for n in range(2):
                ycp[way, (n + 2) % 4 if way == 0 else n].wait_recv()

    def y_finish():
        for way in (0, 1):
            for n in range(2):
                ycp[way, 4 + n].wait_recv()

    lane = lax.broadcasted_iota(jnp.int32, (tok_dev, 128), 1)
    token_i = lax.broadcasted_iota(jnp.int32, (tok_dev, tok_dev), 0)
    token_j = lax.broadcasted_iota(jnp.int32, (tok_dev, tok_dev), 1)
    token_f = lax.broadcasted_iota(jnp.int32, (tok_dev, 128), 0).astype(F32)
    slot_f = (lane % CAP).astype(F32)
    expert_x = ((lane % 64) // 16) * nz
    earlier = jnp.where(token_j < token_i, 1.0, 0.0).astype(BF16)

    def column(row):
        picked = jnp.where(token_i == token_j, jnp.broadcast_to(row, (tok_dev, tok_dev)), 0.0)
        return jnp.broadcast_to(jnp.sum(picked, axis=1, keepdims=True), (tok_dev, 128))

    for c in named:
        c.wait()
    routes = [column(routes_ref[k : k + 1, :].astype(F32)) for k in range(top)]
    combine = [column(combine_ref[k : k + 1, :]) for k in range(top)]

    def table_row(zz):
        wanted = (expert_x + zz).astype(F32)
        member = jnp.zeros((tok_dev, 128), F32)
        weight = jnp.zeros((tok_dev, 128), F32)
        for k in range(top):
            hit = routes[k] == wanted
            member = jnp.where(hit, 1.0, member)
            weight = jnp.where(hit, combine[k], weight)
        rank = jnp.dot(earlier, member.astype(BF16), preferred_element_type=F32)
        chosen = jnp.where(rank == slot_f, member, 0.0)
        value = jnp.where(lane < 64, token_f + 1.0, weight)
        total = jnp.sum(chosen * value, axis=0, keepdims=True)
        zm[pairs, 0, pl.ds(zz, 1), :] = jnp.where(lane[:1] < 64, total - 1.0, total)

    def table_rows(i, carry):
        for j in range(4):
            table_row(i * 4 + j)
        return carry

    lax.fori_loop(0, nz // 4, table_rows, 0)

    z_start(tables + cotangents, 1)

    srow = lax.broadcasted_iota(jnp.int32, (64, 128), 0)
    slane = lax.broadcasted_iota(jnp.int32, (64, 128), 1)
    upper = ((srow[:, :1] // 8) % 2).astype(F32)
    chunk = min(512, dim)
    chunks = dim // chunk

    def columns_of(m):
        m = jnp.broadcast_to(m, (64, 128))
        index_col = jnp.sum(jnp.where(slane == srow, m, 0.0), axis=1, keepdims=True)
        weight_col = jnp.sum(jnp.where(slane == srow + 64, m, 0.0), axis=1, keepdims=True)
        return index_col, weight_col

    def one_hot(index_col, width):
        tokens = lax.broadcasted_iota(jnp.int32, (64, width), 1).astype(F32)
        return jnp.where(index_col == tokens, 1.0, 0.0).astype(BF16)

    def pick_of(g):
        p = g - 1
        ma = zm[p, 0, pl.ds(z, 1), :]
        mb = zm[p, 1, pl.ds(z, 1), :]
        index_col, weight_col = columns_of(jnp.where((slane[:1] // 8) % 2 == 0, ma, mb))
        index_col = jnp.where(index_col >= 0.0, index_col + upper * tok_dev, -1.0)
        return one_hot(index_col, 2 * tok_dev), weight_col

    def select_rows(g, pick):
        def body(n, carry):
            cols = pl.ds(pl.multiple_of(n * chunk, chunk), chunk)
            rows = zx[g - 1, :, :, cols].reshape(2 * tok_dev, chunk)
            got = jnp.dot(pick, rows, preferred_element_type=F32).astype(BF16)
            sx[g, :, :, cols] = got.reshape(NX, 16, chunk)
            return carry

        lax.fori_loop(0, chunks, body, 0)

    def select_grads(g, pick, weight_col):
        def body(n, carry):
            cols = pl.ds(pl.multiple_of(n * chunk, chunk), chunk)
            grads = zc[g - 1, :, :, cols].reshape(2 * tok_dev, chunk)
            got = (weight_col * jnp.dot(pick, grads, preferred_element_type=F32)).astype(BF16)
            sg[g - 1, :, :, cols] = got.reshape(NX, 16, chunk)
            return carry

        lax.fori_loop(0, chunks, body, 0)

    def select_one(g, b, first, count):
        index_col, weight_col = columns_of(zm[pairs, b, pl.ds(z, 1), :])
        pick = one_hot(index_col, tok_dev)
        is_grad = jnp.broadcast_to(upper, (64, chunk)) > 0.0

        def body(n, carry):
            cols = pl.ds(pl.multiple_of(n * chunk, chunk), chunk)
            rows = jnp.dot(pick, zx[pairs, b, :, cols], preferred_element_type=F32)
            grads = weight_col * jnp.dot(pick, zc[pairs, b, :, cols], preferred_element_type=F32)
            sx[g, :, :, cols] = jnp.where(is_grad, grads, rows).astype(BF16).reshape(NX, 16, chunk)
            return carry

        lax.fori_loop(first, first + count, body, 0)

    xcp = {}
    x_far, x_next, x_prev = (x + 2) % NX, (x + 1) % NX, (x + 3) % NX

    def x_copy(i, g, src, dst, way):
        xcp[i, g] = send(src, dst, xs_sem.at[i, g], xr_sem.at[i, g], at_x(way))

    def x_stay(i, g, src, dst):
        xcp[i, g] = pltpu.make_async_copy(src, dst, xl_sem.at[i - 8, g])
        xcp[i, g].start()

    def is_pair(g):
        return 1 <= g <= pairs

    def send_rows(g):
        x_copy(0, g, sx.at[g, x_far], lx.at[g], 1)
        x_copy(2, g, sx.at[g, x_next], rx.at[g, 0, 1], 1)
        x_copy(3, g, sx.at[g, x_prev], rx.at[g, 0, 3], -1)
        x_stay(8, g, sx.at[g, x], rx.at[g, 0, 0])

    def send_grads(g):
        x_copy(1, g, sg.at[g - 1, x_far], lg.at[g - 1], -1)
        x_copy(5, g, sg.at[g - 1, x_prev], rg.at[g - 1, 0, 3], -1)
        x_copy(4, g, sg.at[g - 1, x_next], rg.at[g - 1, 0, 1], 1)
        x_stay(9, g, sg.at[g - 1, x], rg.at[g - 1, 0, 0])

    def send_left(g):
        x_copy(0, g, sx.at[g, x_far, :, left_half], lx.at[g, :, left_half], 1)
        x_copy(2, g, sx.at[g, x_next, :, left_half], rx.at[g, 0, 1, :, left_half], 1)
        x_copy(3, g, sx.at[g, x_prev, :, left_half], rx.at[g, 0, 3, :, left_half], -1)
        x_stay(8, g, sx.at[g, x, :, left_half], rx.at[g, 0, 0, :, left_half])

    def send_right(g):
        x_copy(1, g, sx.at[g, x_far, :, right_half], lx.at[g, :, right_half], -1)
        x_copy(5, g, sx.at[g, x_prev, :, right_half], rx.at[g, 0, 3, :, right_half], -1)
        x_copy(4, g, sx.at[g, x_next, :, right_half], rx.at[g, 0, 1, :, right_half], 1)
        x_stay(9, g, sx.at[g, x, :, right_half], rx.at[g, 0, 0, :, right_half])

    def is_pair(g):
        return 1 <= g <= pairs

    def relay_first(g):
        xcp[0, g].wait_recv()
        if is_pair(g):
            x_copy(6, g, lx.at[g], rx.at[g, 0, 2], 1)
        else:
            x_copy(6, g, lx.at[g, :, left_half], rx.at[g, 0, 2, :, left_half], 1)

    def relay_second(g):
        xcp[1, g].wait_recv()
        if is_pair(g):
            x_copy(7, g, lg.at[g - 1], rg.at[g - 1, 0, 2], -1)
        else:
            x_copy(7, g, lx.at[g, :, right_half], rx.at[g, 0, 2, :, right_half], -1)

    pcp = {}

    def share(i, g, buf, h, cols=slice(None)):
        pcp[i, g] = send(
            buf.at[h, 0, :, :, cols], buf.at[h, 1, :, :, cols], ps_sem.at[i, g], pr_sem.at[i, g], partner
        )

    def share_first(g):
        xcp[8, g].wait()
        for i in (2, 3, 6):
            xcp[i, g].wait_recv()
        if is_pair(g):
            share(0, g, rx, g)
        else:
            share(0, g, rx, g, left_half)

    def share_second(g):
        xcp[9, g].wait()
        for i in (4, 5, 7):
            xcp[i, g].wait_recv()
        if is_pair(g):
            share(1, g, rg, g - 1)
        else:
            share(1, g, rx, g, right_half)

    def arrived(g, n):
        for i in range(g, g + n):
            pcp[0, i].wait_recv()
            pcp[1, i].wait_recv()

    def times(lhs, rows):
        return lax.dot_general(lhs, rows, (((1,), (1,)), ((), ())), preferred_element_type=F32)

    def pointwise(g, at, width, single, qa, qb):
        def body(i, carry):
            q = qa + i // 2
            rows = pl.ds(pl.multiple_of((i % 2) * (hs // 2), hs // 2), hs // 2)
            pre_gate, pre_up, tan_gate, tan_up, back = [proj[q, k, rows, pl.ds(at, width)] for k in range(5)]
            if single:
                back = pltpu.roll(back, width - CAP, 1)
                is_row = (lax.broadcasted_iota(jnp.int32, (hs // 2, width), 1) // CAP) % 2 == 0
                back = jnp.where(is_row, back, 0.0)
            sig = 1.0 / (1.0 + jnp.exp(-pre_gate))
            first = sig * (1.0 + pre_gate * (1.0 - sig))
            second = sig * (1.0 - sig) * (2.0 + pre_gate * (1.0 - 2.0 * sig))
            cols = pl.ds(g * rows_of, width)
            dirs[q, 0, rows, cols] = (back * (tan_up * first + pre_up * second * tan_gate)).astype(BF16)
            dirs[q, 1, rows, cols] = (back * first * tan_gate).astype(BF16)
            return carry

        lax.fori_loop(0, 2 * (qb - qa), body, 0)

    def terms(g, n, qa, qb):
        width = n * rows_of
        slices = qb - qa

        got = times(wbuf[qa:qb, :4].reshape(slices * 4 * hs, dim), rx[g : g + n].reshape(width, dim))
        proj[qa:qb, :4, :, pl.ds(0, width)] = got.reshape(slices, 4, hs, width)
        down = wbuf[qa:qb, 4].reshape(slices * hs, dim)
        singles = 0 if is_pair(g) else rows_of
        if singles:
            got = times(down, rx[g].reshape(rows_of, dim))
            proj[qa:qb, 4, :, pl.ds(0, rows_of)] = got.reshape(slices, hs, rows_of)
            pointwise(g, 0, rows_of, True, qa, qb)
            g = g + 1
        rest = width - singles
        if rest:
            got = times(down, rg[g - 1 : g - 1 + rest // rows_of].reshape(rest, dim))
            proj[qa:qb, 4, :, pl.ds(singles, rest)] = got.reshape(slices, hs, rest)
            pointwise(g, singles, rest, False, qa, qb)

    def early_product(qa, qb, first, count, add):
        depth = count * rows_of
        slices = qb - qa
        wide = chunk if slices == 1 else chunk // 2

        def body(i, carry):
            cols = pl.ds(pl.multiple_of(i * wide, wide), wide)
            rows = rx[first : first + count, :, :, :, cols].reshape(depth, wide)
            d = dirs[qa:qb, :, :, pl.ds(first * rows_of, depth)].reshape(slices * 2 * hs, depth)
            value = jnp.dot(d, rows, preferred_element_type=F32).reshape(slices, 2, hs, wide)
            part[qa:qb, :, :, cols] = part[qa:qb, :, :, cols] + value if add else value
            return carry

        lax.fori_loop(0, dim // wide, body, 0)

    def last_product(q, first, count):
        depth = count * rows_of

        def body(n, carry):
            cols = pl.ds(pl.multiple_of(n * chunk, chunk), chunk)
            rows = rx[first : first + count, :, :, :, cols].reshape(depth, chunk)
            d = dirs[q, :, :, pl.ds(first * rows_of, depth)].reshape(2 * hs, depth)
            acc = part[q, :, :, cols] + jnp.dot(d, rows, preferred_element_type=F32).reshape(2, hs, chunk)
            gate, up = acc[0], acc[1]
            if q == QFAR:
                sb[0, :, cols] = gate.astype(BF16)
                sb[1, :, cols] = up.astype(BF16)
            elif q == QNEXT:
                part[q, 0, :, cols] = gate
                sb[2, :, cols] = up.astype(BF16)
            elif q == QPREV:
                sb[3, :, cols] = gate.astype(BF16)
                part[q, 1, :, cols] = up
            else:
                part[q, :, :, cols] = acc
            return carry

        lax.fori_loop(0, chunks, body, 0)

    rcp = {}

    def r_send(i, src, dst, way):
        rcp[i] = send(sb.at[src], dst, rs_sem.at[i], rr_sem.at[i], at_y(way))

    local[0].wait()
    local[1].wait()
    select_one(own, 0, 0, chunks)
    send_left(own)
    send_right(own)
    for s in range(1, steps):
        z_wait(tokens + tables, s)
        pick, weight_col = pick_of(s)
        select_rows(s, pick)
        send_rows(s)
        relay_first(s - 1)
        if s >= 2:
            share_first(s - 2)
        if s == steps - 2:
            y_near()
            arrived(own, 2)
            terms(own, 2, QNEXT, 4)
        if s == steps - 1:
            early_product(QNEXT, 4, own, 4, False)
        z_wait(cotangents, s)
        select_grads(s, pick, weight_col)
        send_grads(s)
        relay_second(s - 1)
        if s >= 2:
            share_second(s - 2)
        if s == 3:
            y_forward()
        if s == steps - 2:
            arrived(2, 2)
            terms(2, 2, QNEXT, 4)
    arrived(4, 2)
    terms(4, 2, QNEXT, 4)
    z_wait(far_lanes[1] + far_lanes[0], steps)
    select_one(far, 1, 0, chunks // 2)
    send_left(far)
    relay_first(pairs)
    share_first(pairs - 1)
    z_wait(far_lanes[2], steps)
    select_one(far, 1, chunks // 2, chunks // 2)
    send_right(far)
    relay_second(pairs)
    share_second(pairs - 1)
    y_finish()
    for g in (own, 2, 4):
        terms(g, 2, QFAR, QNEXT)
    relay_first(far)
    relay_second(far)
    share_first(pairs)
    share_second(pairs)
    early_product(QFAR, QNEXT, own, 6, False)
    early_product(QNEXT, 4, 4, 2, True)
    arrived(6, 2)
    terms(6, 2, QFAR, QNEXT)
    share_first(far)
    share_second(far)
    terms(6, 2, QNEXT, QPREV)
    arrived(far, 1)
    terms(far, 1, QFAR, QNEXT)
    last_product(QFAR, 6, 3)
    r_send(0, 0, rb.at[0], 1)
    r_send(1, 1, rb.at[1], -1)
    terms(6, 2, QPREV, 4)
    terms(far, 1, QNEXT, 4)
    last_product(QNEXT, 6, 3)
    r_send(2, 2, theirs_hbm.at[0, 0, 1], 1)
    last_product(QPREV, 6, 3)
    r_send(3, 3, theirs_hbm.at[1, 0, 0], -1)
    last_product(QOWN, 6, 3)
    keep = pltpu.make_async_copy(part.at[QOWN], mine_hbm.at[0], loc_sem.at[0])
    keep.start()
    rcp[0].wait_recv()
    sb[4] = (part[QNEXT, 0] + rb[0].astype(F32)).astype(BF16)
    r_send(4, 4, theirs_hbm.at[0, 0, 0], 1)
    rcp[1].wait_recv()
    sb[5] = (part[QPREV, 1] + rb[1].astype(F32)).astype(BF16)
    r_send(5, 5, theirs_hbm.at[1, 0, 1], -1)
    keep.wait()
    for i in range(2, 6):
        rcp[i].wait_recv()
    for c in sent:
        c.wait_send()


def local(tokens, cotangent, routes, combine, w_in, w_out, v_in):
    nz = lax.axis_size("expert") // NX
    pairs = nz // 2 - 1
    groups = pairs + 2
    tok_dev, dim = tokens.shape
    hs = w_out.shape[1]
    top = routes.shape[1]
    rows_of = 2 * NX * 16
    any_spec = pl.BlockSpec(memory_space=pl.ANY)
    dma = pltpu.SemaphoreType.DMA
    mine, theirs = pl.pallas_call(
        functools.partial(kernel, nz),
        out_shape=(
            jax.ShapeDtypeStruct((1, 2, hs, dim), F32),
            jax.ShapeDtypeStruct((2, 1, 2, hs, dim), BF16),
        ),
        in_specs=[pl.BlockSpec(memory_space=pltpu.HBM)] * 7,
        out_specs=(any_spec, any_spec),
        scratch_shapes=[
            pltpu.VMEM((top, tok_dev), jnp.int32),
            pltpu.VMEM((top, tok_dev), F32),
            pltpu.VMEM((pairs + 1, 2, tok_dev, dim), BF16),
            pltpu.VMEM((pairs + 1, 2, tok_dev, dim), BF16),
            pltpu.VMEM((pairs + 1, 2, nz, 128), F32),
            pltpu.VMEM((groups, NX, 16, dim), BF16),
            pltpu.VMEM((pairs, NX, 16, dim), BF16),
            pltpu.VMEM((groups, 16, dim), BF16),
            pltpu.VMEM((pairs, 16, dim), BF16),
            pltpu.VMEM((groups, 2, NX, 16, dim), BF16),
            pltpu.VMEM((pairs, 2, NX, 16, dim), BF16),
            pltpu.VMEM((4, 5, hs, dim), BF16),
            pltpu.VMEM((4, 5, hs, 2 * rows_of), F32),
            pltpu.VMEM((4, 2, hs, groups * rows_of), BF16),
            pltpu.VMEM((4, 2, hs, dim), F32),
            pltpu.VMEM((6, hs, dim), BF16),
            pltpu.VMEM((2, hs, dim), BF16),
            dma((7,)),
            dma((2, 4, pairs + 1)),
            dma((2, 4, pairs + 1)),
            dma((2, 6)),
            dma((2, 6)),
            dma((8, groups)),
            dma((8, groups)),
            dma((2, groups)),
            dma((2, groups)),
            dma((2, groups)),
            dma((6,)),
            dma((6,)),
        ],
        compiler_params=pltpu.CompilerParams(
            collective_id=0, has_side_effects=True, vmem_limit_bytes=50 * 1024 * 1024
        ),
    )(*[pltpu.with_memory_space_constraint(v, pltpu.HBM) for v in (tokens, cotangent, routes.T, combine.T, w_in, w_out, v_in)])
    return mine + theirs[0].astype(F32) + theirs[1].astype(F32)


def solution(mesh):
    in_specs = (
        P(("dp", "expert"), None),
        P(("dp", "expert"), None),
        P(("dp", "expert"), None),
        P(("dp", "expert"), None),
        P("expert", None, "dp", None),
        P("expert", "dp", None),
        P("expert", None, "dp", None),
    )
    out_specs = P("expert", None, "dp", None)
    return jax.shard_map(local, mesh=mesh, in_specs=in_specs, out_specs=out_specs, check_vma=False)
```

```python
import functools

import jax
import jax.numpy as jnp
from jax import lax
from jax.experimental import pallas as pl
from jax.experimental.pallas import tpu as pltpu
from jax.sharding import PartitionSpec as P

MESH = pl.DeviceIdType.MESH
F32 = jnp.float32
BF16 = jnp.bfloat16
NX = 4
NY = 4
NC = 2
CAP = 8
QFAR, QNEXT, QPREV, QOWN = 0, 1, 2, 3


def kernel(
    nz, tok_hbm, cot_hbm, routes_hbm, combine_hbm, win_hbm, wout_hbm, vin_hbm, mine_hbm, theirs_hbm,
    routes_ref, combine_ref, zx, zc, zm, sx, sg, lx, lg, rx, rg, wbuf, proj, dirs, part, sb, rb,
    loc_sem, zs_sem, zr_sem, ys_sem, yr_sem, xs_sem, xr_sem, xl_sem, ps_sem, pr_sem, rs_sem, rr_sem,
):
    steps = nz // 2
    pairs = steps - 1
    own, far = 0, pairs + 1
    tok_dev, dim = tok_hbm.shape
    top = routes_hbm.shape[0]
    hs = wout_hbm.shape[1]
    rows_of = 2 * NX * 16
    dp = lax.axis_index("dp")
    ex = lax.axis_index("expert")
    y, core = dp // NC, dp % NC
    x, z = ex // nz, ex % nz

    def at_z(k):
        return (dp, x * nz + (z + k + nz) % nz)

    def at_x(k):
        return (dp, ((x + k + NX) % NX) * nz + z)

    def at_y(k):
        return (((y + k + NY) % NY) * NC + core, ex)

    partner = (y * NC + (1 - core), ex)

    barrier = pltpu.get_barrier_semaphore()
    neighbours = [at_z(1), at_z(-1), at_x(1), at_x(-1), at_y(1), at_y(-1), partner]
    for n in neighbours:
        pl.semaphore_signal(barrier, inc=1, device_id=n, device_id_type=MESH)

    named = [
        pltpu.make_async_copy(routes_hbm, routes_ref, loc_sem.at[5]),
        pltpu.make_async_copy(combine_hbm, combine_ref, loc_sem.at[6]),
    ]
    local = [
        pltpu.make_async_copy(tok_hbm, zx.at[pairs, 0], loc_sem.at[0]),
        pltpu.make_async_copy(cot_hbm, zc.at[pairs, 0], loc_sem.at[1]),
        pltpu.make_async_copy(win_hbm.at[0], wbuf.at[QOWN, pl.ds(0, 2)], loc_sem.at[2]),
        pltpu.make_async_copy(vin_hbm.at[0], wbuf.at[QOWN, pl.ds(2, 2)], loc_sem.at[3]),
        pltpu.make_async_copy(wout_hbm.at[0], wbuf.at[QOWN, 4], loc_sem.at[4]),
    ]
    for c in named + local:
        c.start()
    pl.semaphore_wait(barrier, len(neighbours))

    sent = []

    def send(src, dst, ssem, rsem, device):
        c = pltpu.make_async_remote_copy(
            src_ref=src, dst_ref=dst, send_sem=ssem, recv_sem=rsem, device_id=device, device_id_type=MESH
        )
        c.start()
        sent.append(c)
        return c

    left_half, right_half = pl.ds(0, dim // 2), pl.ds(dim // 2, dim // 2)
    zbuf = (zx, zc, zm)

    def z_send(way, kind, s):
        part_of = slice(None)
        buf = zbuf[way if kind == 3 else kind]
        if s == steps and kind != 2:
            part_of = right_half if kind == 3 else left_half
        dst = (s - 1, way) if s < steps else (pairs, 1)
        if s > 1:
            src = buf.at[s - 2, way, :, part_of]
        elif kind == 2:
            src = buf.at[pairs, 0]
        else:
            src = (tok_hbm, cot_hbm)[kind]
        return send(
            src, buf.at[dst[0], dst[1], :, part_of], zs_sem.at[way, kind, s - 1], zr_sem.at[way, kind, s - 1],
            at_z(1 if way == 0 else -1),
        )

    tables, tokens, cotangents = [(0, 2), (1, 2)], [(0, 0), (1, 0)], [(0, 1), (1, 1)]
    far_lanes = [(0, 2)], [(0, 0), (1, 1)], [(0, 3), (1, 3)]
    zcp = {}

    def z_start(lanes, s):
        for way, kind in lanes:
            zcp[way, kind, s] = z_send(way, kind, s)

    def z_wait(lanes, s):
        for way, kind in lanes:
            zcp[way, kind, s].wait_recv()
            if s < steps - 1:
                z_start([(way, kind)], s + 1)
            elif s == steps - 1:
                if (way, kind) in ((0, 0), (1, 1)):
                    z_start([(way, kind), (way, 3)], s + 1)
                elif (way, kind) == (0, 2):
                    z_start([(way, kind)], s + 1)

    z_start(tokens, 1)

    half_rows = hs // 2

    def piece(q, i):
        if i == 0:
            return wbuf.at[q, pl.ds(0, 2)]
        if i == 1:
            return wbuf.at[q, 4, pl.ds(0, half_rows)]
        if i == 2:
            return wbuf.at[q, pl.ds(2, 2)]
        return wbuf.at[q, 4, pl.ds(half_rows, half_rows)]

    own_piece = (
        win_hbm.at[0], wout_hbm.at[0, pl.ds(0, half_rows)], vin_hbm.at[0], wout_hbm.at[0, pl.ds(half_rows, half_rows)]
    )
    ycp = {}
    for n in range(4):
        for way in (0, 1):
            i = n if way == 0 else (n + 2) % 4
            ycp[way, i] = send(
                own_piece[i], piece(QPREV if way == 0 else QNEXT, i),
                ys_sem.at[way, i], yr_sem.at[way, i], at_y(1 if way == 0 else -1),
            )

    def y_forward():
        for n in range(2):
            for way in (0, 1):
                i = n if way == 0 else n + 2
                ycp[way, i].wait_recv()
                ycp[way, 4 + n] = send(
                    piece(QPREV if way == 0 else QNEXT, i), piece(QFAR, i),
                    ys_sem.at[way, 4 + n], yr_sem.at[way, 4 + n], at_y(1 if way == 0 else -1),
                )

    def y_near():
        for c in local[2:]:
            c.wait()
        for way in (0, 1):
            for n in range(2):
                ycp[way, (n + 2) % 4 if way == 0 else n].wait_recv()

    def y_finish():
        for way in (0, 1):
            for n in range(2):
                ycp[way, 4 + n].wait_recv()

    lane = lax.broadcasted_iota(jnp.int32, (tok_dev, 128), 1)
    token_i = lax.broadcasted_iota(jnp.int32, (tok_dev, tok_dev), 0)
    token_j = lax.broadcasted_iota(jnp.int32, (tok_dev, tok_dev), 1)
    token_f = lax.broadcasted_iota(jnp.int32, (tok_dev, 128), 0).astype(F32)
    slot_f = (lane % CAP).astype(F32)
    expert_x = ((lane % 64) // 16) * nz
    earlier = jnp.where(token_j < token_i, 1.0, 0.0).astype(BF16)

    def column(row):
        picked = jnp.where(token_i == token_j, jnp.broadcast_to(row, (tok_dev, tok_dev)), 0.0)
        return jnp.broadcast_to(jnp.sum(picked, axis=1, keepdims=True), (tok_dev, 128))

    for c in named:
        c.wait()
    routes = [column(routes_ref[k : k + 1, :].astype(F32)) for k in range(top)]
    combine = [column(combine_ref[k : k + 1, :]) for k in range(top)]

    def table_row(zz):
        wanted = (expert_x + zz).astype(F32)
        member = jnp.zeros((tok_dev, 128), F32)
        weight = jnp.zeros((tok_dev, 128), F32)
        for k in range(top):
            hit = routes[k] == wanted
            member = jnp.where(hit, 1.0, member)
            weight = jnp.where(hit, combine[k], weight)
        rank = jnp.dot(earlier, member.astype(BF16), preferred_element_type=F32)
        chosen = jnp.where(rank == slot_f, member, 0.0)
        value = jnp.where(lane < 64, token_f + 1.0, weight)
        total = jnp.sum(chosen * value, axis=0, keepdims=True)
        zm[pairs, 0, pl.ds(zz, 1), :] = jnp.where(lane[:1] < 64, total - 1.0, total)

    def table_rows(i, carry):
        for j in range(4):
            table_row(i * 4 + j)
        return carry

    lax.fori_loop(0, nz // 4, table_rows, 0)

    z_start(tables + cotangents, 1)

    srow = lax.broadcasted_iota(jnp.int32, (64, 128), 0)
    slane = lax.broadcasted_iota(jnp.int32, (64, 128), 1)
    upper = ((srow[:, :1] // 8) % 2).astype(F32)
    chunk = min(512, dim)
    chunks = dim // chunk

    def columns_of(m):
        m = jnp.broadcast_to(m, (64, 128))
        index_col = jnp.sum(jnp.where(slane == srow, m, 0.0), axis=1, keepdims=True)
        weight_col = jnp.sum(jnp.where(slane == srow + 64, m, 0.0), axis=1, keepdims=True)
        return index_col, weight_col

    def one_hot(index_col, width):
        tokens = lax.broadcasted_iota(jnp.int32, (64, width), 1).astype(F32)
        return jnp.where(index_col == tokens, 1.0, 0.0).astype(BF16)

    def pick_of(g):
        p = g - 1
        ma = zm[p, 0, pl.ds(z, 1), :]
        mb = zm[p, 1, pl.ds(z, 1), :]
        index_col, weight_col = columns_of(jnp.where((slane[:1] // 8) % 2 == 0, ma, mb))
        index_col = jnp.where(index_col >= 0.0, index_col + upper * tok_dev, -1.0)
        return one_hot(index_col, 2 * tok_dev), weight_col

    def select_rows(g, pick):
        def body(n, carry):
            cols = pl.ds(pl.multiple_of(n * chunk, chunk), chunk)
            rows = zx[g - 1, :, :, cols].reshape(2 * tok_dev, chunk)
            got = jnp.dot(pick, rows, preferred_element_type=F32).astype(BF16)
            sx[g, :, :, cols] = got.reshape(NX, 16, chunk)
            return carry

        lax.fori_loop(0, chunks, body, 0)

    def select_grads(g, pick, weight_col):
        def body(n, carry):
            cols = pl.ds(pl.multiple_of(n * chunk, chunk), chunk)
            grads = zc[g - 1, :, :, cols].reshape(2 * tok_dev, chunk)
            got = (weight_col * jnp.dot(pick, grads, preferred_element_type=F32)).astype(BF16)
            sg[g - 1, :, :, cols] = got.reshape(NX, 16, chunk)
            return carry

        lax.fori_loop(0, chunks, body, 0)

    def select_one(g, b, first, count):
        index_col, weight_col = columns_of(zm[pairs, b, pl.ds(z, 1), :])
        pick = one_hot(index_col, tok_dev)
        is_grad = jnp.broadcast_to(upper, (64, chunk)) > 0.0

        def body(n, carry):
            cols = pl.ds(pl.multiple_of(n * chunk, chunk), chunk)
            rows = jnp.dot(pick, zx[pairs, b, :, cols], preferred_element_type=F32)
            grads = weight_col * jnp.dot(pick, zc[pairs, b, :, cols], preferred_element_type=F32)
            sx[g, :, :, cols] = jnp.where(is_grad, grads, rows).astype(BF16).reshape(NX, 16, chunk)
            return carry

        lax.fori_loop(first, first + count, body, 0)

    xcp = {}
    x_far, x_next, x_prev = (x + 2) % NX, (x + 1) % NX, (x + 3) % NX

    def x_copy(i, g, src, dst, way):
        xcp[i, g] = send(src, dst, xs_sem.at[i, g], xr_sem.at[i, g], at_x(way))

    def x_stay(i, g, src, dst):
        xcp[i, g] = pltpu.make_async_copy(src, dst, xl_sem.at[i - 8, g])
        xcp[i, g].start()

    def is_pair(g):
        return 1 <= g <= pairs

    def send_rows(g):
        x_copy(0, g, sx.at[g, x_far], lx.at[g], 1)
        x_copy(2, g, sx.at[g, x_next], rx.at[g, 0, 1], 1)
        x_copy(3, g, sx.at[g, x_prev], rx.at[g, 0, 3], -1)
        x_stay(8, g, sx.at[g, x], rx.at[g, 0, 0])

    def send_grads(g):
        x_copy(1, g, sg.at[g - 1, x_far], lg.at[g - 1], -1)
        x_copy(5, g, sg.at[g - 1, x_prev], rg.at[g - 1, 0, 3], -1)
        x_copy(4, g, sg.at[g - 1, x_next], rg.at[g - 1, 0, 1], 1)
        x_stay(9, g, sg.at[g - 1, x], rg.at[g - 1, 0, 0])

    def send_left(g):
        x_copy(0, g, sx.at[g, x_far, :, left_half], lx.at[g, :, left_half], 1)
        x_copy(2, g, sx.at[g, x_next, :, left_half], rx.at[g, 0, 1, :, left_half], 1)
        x_copy(3, g, sx.at[g, x_prev, :, left_half], rx.at[g, 0, 3, :, left_half], -1)
        x_stay(8, g, sx.at[g, x, :, left_half], rx.at[g, 0, 0, :, left_half])

    def send_right(g):
        x_copy(1, g, sx.at[g, x_far, :, right_half], lx.at[g, :, right_half], -1)
        x_copy(5, g, sx.at[g, x_prev, :, right_half], rx.at[g, 0, 3, :, right_half], -1)
        x_copy(4, g, sx.at[g, x_next, :, right_half], rx.at[g, 0, 1, :, right_half], 1)
        x_stay(9, g, sx.at[g, x, :, right_half], rx.at[g, 0, 0, :, right_half])

    def is_pair(g):
        return 1 <= g <= pairs

    def relay_first(g):
        xcp[0, g].wait_recv()
        if is_pair(g):
            x_copy(6, g, lx.at[g], rx.at[g, 0, 2], 1)
        else:
            x_copy(6, g, lx.at[g, :, left_half], rx.at[g, 0, 2, :, left_half], 1)

    def relay_second(g):
        xcp[1, g].wait_recv()
        if is_pair(g):
            x_copy(7, g, lg.at[g - 1], rg.at[g - 1, 0, 2], -1)
        else:
            x_copy(7, g, lx.at[g, :, right_half], rx.at[g, 0, 2, :, right_half], -1)

    pcp = {}

    def share(i, g, buf, h, cols=slice(None)):
        pcp[i, g] = send(
            buf.at[h, 0, :, :, cols], buf.at[h, 1, :, :, cols], ps_sem.at[i, g], pr_sem.at[i, g], partner
        )

    def share_first(g):
        xcp[8, g].wait()
        for i in (2, 3, 6):
            xcp[i, g].wait_recv()
        if is_pair(g):
            share(0, g, rx, g)
        else:
            share(0, g, rx, g, left_half)

    def share_second(g):
        xcp[9, g].wait()
        for i in (4, 5, 7):
            xcp[i, g].wait_recv()
        if is_pair(g):
            share(1, g, rg, g - 1)
        else:
            share(1, g, rx, g, right_half)

    def arrived(g, n):
        for i in range(g, g + n):
            pcp[0, i].wait_recv()
            pcp[1, i].wait_recv()

    def times(lhs, rows):
        return lax.dot_general(lhs, rows, (((1,), (1,)), ((), ())), preferred_element_type=F32)

    def pointwise(g, at, width, single, qa, qb):
        def body(i, carry):
            q = qa + i // 2
            rows = pl.ds(pl.multiple_of((i % 2) * (hs // 2), hs // 2), hs // 2)
            pre_gate, pre_up, tan_gate, tan_up, back = [proj[q, k, rows, pl.ds(at, width)] for k in range(5)]
            if single:
                back = pltpu.roll(back, width - CAP, 1)
                is_row = (lax.broadcasted_iota(jnp.int32, (hs // 2, width), 1) // CAP) % 2 == 0
                back = jnp.where(is_row, back, 0.0)
            sig = 1.0 / (1.0 + jnp.exp(-pre_gate))
            first = sig * (1.0 + pre_gate * (1.0 - sig))
            second = sig * (1.0 - sig) * (2.0 + pre_gate * (1.0 - 2.0 * sig))
            cols = pl.ds(g * rows_of, width)
            dirs[q, 0, rows, cols] = (back * (tan_up * first + pre_up * second * tan_gate)).astype(BF16)
            dirs[q, 1, rows, cols] = (back * first * tan_gate).astype(BF16)
            return carry

        lax.fori_loop(0, 2 * (qb - qa), body, 0)

    def terms(g, n, qa, qb):
        width = n * rows_of
        slices = qb - qa

        got = times(wbuf[qa:qb, :4].reshape(slices * 4 * hs, dim), rx[g : g + n].reshape(width, dim))
        proj[qa:qb, :4, :, pl.ds(0, width)] = got.reshape(slices, 4, hs, width)
        down = wbuf[qa:qb, 4].reshape(slices * hs, dim)
        singles = 0 if is_pair(g) else rows_of
        if singles:
            got = times(down, rx[g].reshape(rows_of, dim))
            proj[qa:qb, 4, :, pl.ds(0, rows_of)] = got.reshape(slices, hs, rows_of)
            pointwise(g, 0, rows_of, True, qa, qb)
            g = g + 1
        rest = width - singles
        if rest:
            got = times(down, rg[g - 1 : g - 1 + rest // rows_of].reshape(rest, dim))
            proj[qa:qb, 4, :, pl.ds(singles, rest)] = got.reshape(slices, hs, rest)
            pointwise(g, singles, rest, False, qa, qb)

    def early_product(qa, qb, first, count, add):
        depth = count * rows_of
        slices = qb - qa
        wide = chunk if slices == 1 else chunk // 2

        def body(i, carry):
            cols = pl.ds(pl.multiple_of(i * wide, wide), wide)
            rows = rx[first : first + count, :, :, :, cols].reshape(depth, wide)
            d = dirs[qa:qb, :, :, pl.ds(first * rows_of, depth)].reshape(slices * 2 * hs, depth)
            value = jnp.dot(d, rows, preferred_element_type=F32).reshape(slices, 2, hs, wide)
            part[qa:qb, :, :, cols] = part[qa:qb, :, :, cols] + value if add else value
            return carry

        lax.fori_loop(0, dim // wide, body, 0)

    def last_product(q, first, count, n_first=0, n_last=chunks):
        depth = count * rows_of

        def body(n, carry):
            cols = pl.ds(pl.multiple_of(n * chunk, chunk), chunk)
            rows = rx[first : first + count, :, :, :, cols].reshape(depth, chunk)
            d = dirs[q, :, :, pl.ds(first * rows_of, depth)].reshape(2 * hs, depth)
            acc = part[q, :, :, cols] + jnp.dot(d, rows, preferred_element_type=F32).reshape(2, hs, chunk)
            gate, up = acc[0], acc[1]
            if q == QFAR:
                sb[0, :, cols] = gate.astype(BF16)
                sb[1, :, cols] = up.astype(BF16)
            elif q == QNEXT:
                part[q, 0, :, cols] = gate
                sb[2, :, cols] = up.astype(BF16)
            elif q == QPREV:
                sb[3, :, cols] = gate.astype(BF16)
                part[q, 1, :, cols] = up
            else:
                part[q, :, :, cols] = acc
            return carry

        lax.fori_loop(n_first, n_last, body, 0)

    rcp = {}

    def r_send(i, src, dst, way, cols=slice(None)):
        rcp[i] = send(sb.at[src, :, cols], dst, rs_sem.at[i], rr_sem.at[i], at_y(way))

    local[0].wait()
    local[1].wait()
    select_one(own, 0, 0, chunks)
    send_left(own)
    send_right(own)
    for s in range(1, steps):
        z_wait(tokens + tables, s)
        pick, weight_col = pick_of(s)
        select_rows(s, pick)
        send_rows(s)
        relay_first(s - 1)
        if s >= 2:
            share_first(s - 2)
        if s == steps - 2:
            y_near()
            arrived(own, 2)
            terms(own, 2, QNEXT, 4)
        if s == steps - 1:
            early_product(QNEXT, 4, own, 4, False)
        z_wait(cotangents, s)
        select_grads(s, pick, weight_col)
        send_grads(s)
        relay_second(s - 1)
        if s >= 2:
            share_second(s - 2)
        if s == 3:
            y_forward()
        if s == steps - 2:
            arrived(2, 2)
            terms(2, 2, QNEXT, 4)
    arrived(4, 2)
    terms(4, 2, QNEXT, 4)
    z_wait(far_lanes[1] + far_lanes[0], steps)
    select_one(far, 1, 0, chunks // 2)
    send_left(far)
    relay_first(pairs)
    share_first(pairs - 1)
    z_wait(far_lanes[2], steps)
    select_one(far, 1, chunks // 2, chunks // 2)
    send_right(far)
    relay_second(pairs)
    share_second(pairs - 1)
    y_finish()
    for g in (own, 2, 4):
        terms(g, 2, QFAR, QNEXT)
    relay_first(far)
    relay_second(far)
    share_first(pairs)
    share_second(pairs)
    early_product(QFAR, QNEXT, own, 6, False)
    early_product(QNEXT, 4, 4, 2, True)
    arrived(6, 2)
    terms(6, 2, QFAR, QNEXT)
    share_first(far)
    share_second(far)
    terms(6, 2, QNEXT, QPREV)
    arrived(far, 1)
    terms(far, 1, QFAR, QNEXT)
    last_product(QFAR, 6, 3, 0, chunks // 2)
    r_send(0, 0, rb.at[0, :, left_half], 1, left_half)
    r_send(1, 1, rb.at[1, :, left_half], -1, left_half)
    last_product(QFAR, 6, 3, chunks // 2, chunks)
    r_send(6, 0, rb.at[0, :, right_half], 1, right_half)
    r_send(7, 1, rb.at[1, :, right_half], -1, right_half)
    terms(6, 2, QPREV, 4)
    terms(far, 1, QNEXT, 4)
    last_product(QNEXT, 6, 3)
    r_send(2, 2, theirs_hbm.at[0, 0, 1], 1)
    last_product(QPREV, 6, 3)
    r_send(3, 3, theirs_hbm.at[1, 0, 0], -1)
    last_product(QOWN, 6, 3)
    keep = pltpu.make_async_copy(part.at[QOWN], mine_hbm.at[0], loc_sem.at[0])
    keep.start()
    rcp[0].wait_recv()
    rcp[6].wait_recv()
    sb[4] = (part[QNEXT, 0] + rb[0].astype(F32)).astype(BF16)
    r_send(4, 4, theirs_hbm.at[0, 0, 0], 1)
    rcp[1].wait_recv()
    rcp[7].wait_recv()
    sb[5] = (part[QPREV, 1] + rb[1].astype(F32)).astype(BF16)
    r_send(5, 5, theirs_hbm.at[1, 0, 1], -1)
    keep.wait()
    for i in range(2, 6):
        rcp[i].wait_recv()
    for c in sent:
        c.wait_send()


def local(tokens, cotangent, routes, combine, w_in, w_out, v_in):
    nz = lax.axis_size("expert") // NX
    pairs = nz // 2 - 1
    groups = pairs + 2
    tok_dev, dim = tokens.shape
    hs = w_out.shape[1]
    top = routes.shape[1]
    rows_of = 2 * NX * 16
    any_spec = pl.BlockSpec(memory_space=pl.ANY)
    dma = pltpu.SemaphoreType.DMA
    mine, theirs = pl.pallas_call(
        functools.partial(kernel, nz),
        out_shape=(
            jax.ShapeDtypeStruct((1, 2, hs, dim), F32),
            jax.ShapeDtypeStruct((2, 1, 2, hs, dim), BF16),
        ),
        in_specs=[pl.BlockSpec(memory_space=pltpu.HBM)] * 7,
        out_specs=(any_spec, any_spec),
        scratch_shapes=[
            pltpu.VMEM((top, tok_dev), jnp.int32),
            pltpu.VMEM((top, tok_dev), F32),
            pltpu.VMEM((pairs + 1, 2, tok_dev, dim), BF16),
            pltpu.VMEM((pairs + 1, 2, tok_dev, dim), BF16),
            pltpu.VMEM((pairs + 1, 2, nz, 128), F32),
            pltpu.VMEM((groups, NX, 16, dim), BF16),
            pltpu.VMEM((pairs, NX, 16, dim), BF16),
            pltpu.VMEM((groups, 16, dim), BF16),
            pltpu.VMEM((pairs, 16, dim), BF16),
            pltpu.VMEM((groups, 2, NX, 16, dim), BF16),
            pltpu.VMEM((pairs, 2, NX, 16, dim), BF16),
            pltpu.VMEM((4, 5, hs, dim), BF16),
            pltpu.VMEM((4, 5, hs, 2 * rows_of), F32),
            pltpu.VMEM((4, 2, hs, groups * rows_of), BF16),
            pltpu.VMEM((4, 2, hs, dim), F32),
            pltpu.VMEM((6, hs, dim), BF16),
            pltpu.VMEM((2, hs, dim), BF16),
            dma((7,)),
            dma((2, 4, pairs + 1)),
            dma((2, 4, pairs + 1)),
            dma((2, 6)),
            dma((2, 6)),
            dma((8, groups)),
            dma((8, groups)),
            dma((2, groups)),
            dma((2, groups)),
            dma((2, groups)),
            dma((8,)),
            dma((8,)),
        ],
        compiler_params=pltpu.CompilerParams(
            collective_id=0, has_side_effects=True, vmem_limit_bytes=50 * 1024 * 1024
        ),
    )(*[pltpu.with_memory_space_constraint(v, pltpu.HBM) for v in (tokens, cotangent, routes.T, combine.T, w_in, w_out, v_in)])
    return mine + theirs[0].astype(F32) + theirs[1].astype(F32)


def solution(mesh):
    in_specs = (
        P(("dp", "expert"), None),
        P(("dp", "expert"), None),
        P(("dp", "expert"), None),
        P(("dp", "expert"), None),
        P("expert", None, "dp", None),
        P("expert", "dp", None),
        P("expert", None, "dp", None),
    )
    out_specs = P("expert", None, "dp", None)
    return jax.shard_map(local, mesh=mesh, in_specs=in_specs, out_specs=out_specs, check_vma=False)
```

```python
import functools

import jax
import jax.numpy as jnp
from jax import lax
from jax.experimental import pallas as pl
from jax.experimental.pallas import tpu as pltpu
from jax.sharding import PartitionSpec as P

MESH = pl.DeviceIdType.MESH
F32 = jnp.float32
BF16 = jnp.bfloat16
NX = 4
NY = 4
NC = 2
CAP = 8
QFAR, QNEXT, QPREV, QOWN = 0, 1, 2, 3


def kernel(
    nz, tok_hbm, cot_hbm, routes_hbm, combine_hbm, win_hbm, wout_hbm, vin_hbm, mine_hbm, theirs_hbm,
    routes_ref, combine_ref, zx, zc, zm, sx, sg, lx, lg, rx, rg, wbuf, proj, dirs, part, sb, rb,
    loc_sem, zs_sem, zr_sem, ys_sem, yr_sem, xs_sem, xr_sem, xl_sem, ps_sem, pr_sem, rs_sem, rr_sem,
):
    steps = nz // 2
    pairs = steps - 1
    own, far = 0, pairs + 1
    tok_dev, dim = tok_hbm.shape
    top = routes_hbm.shape[0]
    hs = wout_hbm.shape[1]
    rows_of = 2 * NX * 16
    dp = lax.axis_index("dp")
    ex = lax.axis_index("expert")
    y, core = dp // NC, dp % NC
    x, z = ex // nz, ex % nz

    def at_z(k):
        return (dp, x * nz + (z + k + nz) % nz)

    def at_x(k):
        return (dp, ((x + k + NX) % NX) * nz + z)

    def at_y(k):
        return (((y + k + NY) % NY) * NC + core, ex)

    partner = (y * NC + (1 - core), ex)

    barrier = pltpu.get_barrier_semaphore()
    neighbours = [at_z(1), at_z(-1), at_x(1), at_x(-1), at_y(1), at_y(-1), partner]
    for n in neighbours:
        pl.semaphore_signal(barrier, inc=1, device_id=n, device_id_type=MESH)

    named = [
        pltpu.make_async_copy(routes_hbm, routes_ref, loc_sem.at[5]),
        pltpu.make_async_copy(combine_hbm, combine_ref, loc_sem.at[6]),
    ]
    local = [
        pltpu.make_async_copy(tok_hbm, zx.at[pairs, 0], loc_sem.at[0]),
        pltpu.make_async_copy(cot_hbm, zc.at[pairs, 0], loc_sem.at[1]),
        pltpu.make_async_copy(win_hbm.at[0], wbuf.at[QOWN, pl.ds(0, 2)], loc_sem.at[2]),
        pltpu.make_async_copy(vin_hbm.at[0], wbuf.at[QOWN, pl.ds(2, 2)], loc_sem.at[3]),
        pltpu.make_async_copy(wout_hbm.at[0], wbuf.at[QOWN, 4], loc_sem.at[4]),
    ]
    for c in named + local:
        c.start()
    pl.semaphore_wait(barrier, len(neighbours))

    sent = []

    def send(src, dst, ssem, rsem, device):
        c = pltpu.make_async_remote_copy(
            src_ref=src, dst_ref=dst, send_sem=ssem, recv_sem=rsem, device_id=device, device_id_type=MESH
        )
        c.start()
        sent.append(c)
        return c

    left_half, right_half = pl.ds(0, dim // 2), pl.ds(dim // 2, dim // 2)
    zbuf = (zx, zc, zm)

    def z_send(way, kind, s):
        part_of = slice(None)
        buf = zbuf[way if kind == 3 else kind]
        if s == steps and kind != 2:
            part_of = right_half if kind == 3 else left_half
        dst = (s - 1, way) if s < steps else (pairs, 1)
        if s > 1:
            src = buf.at[s - 2, way, :, part_of]
        elif kind == 2:
            src = buf.at[pairs, 0]
        else:
            src = (tok_hbm, cot_hbm)[kind]
        return send(
            src, buf.at[dst[0], dst[1], :, part_of], zs_sem.at[way, kind, s - 1], zr_sem.at[way, kind, s - 1],
            at_z(1 if way == 0 else -1),
        )

    tables, tokens, cotangents = [(0, 2), (1, 2)], [(0, 0), (1, 0)], [(0, 1), (1, 1)]
    far_lanes = [(0, 2)], [(0, 0), (1, 1)], [(0, 3), (1, 3)]
    zcp = {}

    def z_start(lanes, s):
        for way, kind in lanes:
            zcp[way, kind, s] = z_send(way, kind, s)

    def z_wait(lanes, s):
        for way, kind in lanes:
            zcp[way, kind, s].wait_recv()
            if s < steps - 1:
                z_start([(way, kind)], s + 1)
            elif s == steps - 1:
                if (way, kind) in ((0, 0), (1, 1)):
                    z_start([(way, kind), (way, 3)], s + 1)
                elif (way, kind) == (0, 2):
                    z_start([(way, kind)], s + 1)

    z_start(tokens, 1)

    half_rows = hs // 2

    def piece(q, i):
        if i == 0:
            return wbuf.at[q, pl.ds(0, 2)]
        if i == 1:
            return wbuf.at[q, 4, pl.ds(0, half_rows)]
        if i == 2:
            return wbuf.at[q, pl.ds(2, 2)]
        return wbuf.at[q, 4, pl.ds(half_rows, half_rows)]

    own_piece = (
        win_hbm.at[0], wout_hbm.at[0, pl.ds(0, half_rows)], vin_hbm.at[0], wout_hbm.at[0, pl.ds(half_rows, half_rows)]
    )
    ycp = {}
    for n in range(4):
        for way in (0, 1):
            i = n if way == 0 else (n + 2) % 4
            ycp[way, i] = send(
                own_piece[i], piece(QPREV if way == 0 else QNEXT, i),
                ys_sem.at[way, i], yr_sem.at[way, i], at_y(1 if way == 0 else -1),
            )

    def y_forward():
        for n in range(2):
            for way in (0, 1):
                i = n if way == 0 else n + 2
                ycp[way, i].wait_recv()
                ycp[way, 4 + n] = send(
                    piece(QPREV if way == 0 else QNEXT, i), piece(QFAR, i),
                    ys_sem.at[way, 4 + n], yr_sem.at[way, 4 + n], at_y(1 if way == 0 else -1),
                )

    def y_near():
        for c in local[2:]:
            c.wait()
        for way in (0, 1):
            for n in range(2):
                ycp[way, (n + 2) % 4 if way == 0 else n].wait_recv()

    def y_finish():
        for way in (0, 1):
            for n in range(2):
                ycp[way, 4 + n].wait_recv()

    lane = lax.broadcasted_iota(jnp.int32, (tok_dev, 128), 1)
    token_i = lax.broadcasted_iota(jnp.int32, (tok_dev, tok_dev), 0)
    token_j = lax.broadcasted_iota(jnp.int32, (tok_dev, tok_dev), 1)
    token_f = lax.broadcasted_iota(jnp.int32, (tok_dev, 128), 0).astype(F32)
    slot_f = (lane % CAP).astype(F32)
    expert_x = ((lane % 64) // 16) * nz
    earlier = jnp.where(token_j < token_i, 1.0, 0.0).astype(BF16)

    def column(row):
        picked = jnp.where(token_i == token_j, jnp.broadcast_to(row, (tok_dev, tok_dev)), 0.0)
        return jnp.broadcast_to(jnp.sum(picked, axis=1, keepdims=True), (tok_dev, 128))

    for c in named:
        c.wait()
    routes = [column(routes_ref[k : k + 1, :].astype(F32)) for k in range(top)]
    combine = [column(combine_ref[k : k + 1, :]) for k in range(top)]

    def table_row(zz):
        wanted = (expert_x + zz).astype(F32)
        member = jnp.zeros((tok_dev, 128), F32)
        weight = jnp.zeros((tok_dev, 128), F32)
        for k in range(top):
            hit = routes[k] == wanted
            member = jnp.where(hit, 1.0, member)
            weight = jnp.where(hit, combine[k], weight)
        rank = jnp.dot(earlier, member.astype(BF16), preferred_element_type=F32)
        chosen = jnp.where(rank == slot_f, member, 0.0)
        value = jnp.where(lane < 64, token_f + 1.0, weight)
        total = jnp.sum(chosen * value, axis=0, keepdims=True)
        zm[pairs, 0, pl.ds(zz, 1), :] = jnp.where(lane[:1] < 64, total - 1.0, total)

    def table_rows(i, carry):
        for j in range(4):
            table_row(i * 4 + j)
        return carry

    lax.fori_loop(0, nz // 4, table_rows, 0)

    z_start(tables + cotangents, 1)

    srow = lax.broadcasted_iota(jnp.int32, (64, 128), 0)
    slane = lax.broadcasted_iota(jnp.int32, (64, 128), 1)
    upper = ((srow[:, :1] // 8) % 2).astype(F32)
    chunk = min(512, dim)
    chunks = dim // chunk

    def columns_of(m):
        m = jnp.broadcast_to(m, (64, 128))
        index_col = jnp.sum(jnp.where(slane == srow, m, 0.0), axis=1, keepdims=True)
        weight_col = jnp.sum(jnp.where(slane == srow + 64, m, 0.0), axis=1, keepdims=True)
        return index_col, weight_col

    def one_hot(index_col, width):
        tokens = lax.broadcasted_iota(jnp.int32, (64, width), 1).astype(F32)
        return jnp.where(index_col == tokens, 1.0, 0.0).astype(BF16)

    def pick_of(g):
        p = g - 1
        ma = zm[p, 0, pl.ds(z, 1), :]
        mb = zm[p, 1, pl.ds(z, 1), :]
        index_col, weight_col = columns_of(jnp.where((slane[:1] // 8) % 2 == 0, ma, mb))
        index_col = jnp.where(index_col >= 0.0, index_col + upper * tok_dev, -1.0)
        return one_hot(index_col, 2 * tok_dev), weight_col

    def select_rows(g, pick):
        def body(n, carry):
            cols = pl.ds(pl.multiple_of(n * chunk, chunk), chunk)
            rows = zx[g - 1, :, :, cols].reshape(2 * tok_dev, chunk)
            got = jnp.dot(pick, rows, preferred_element_type=F32).astype(BF16)
            sx[g, :, :, cols] = got.reshape(NX, 16, chunk)
            return carry

        lax.fori_loop(0, chunks, body, 0)

    def select_grads(g, pick, weight_col):
        def body(n, carry):
            cols = pl.ds(pl.multiple_of(n * chunk, chunk), chunk)
            grads = zc[g - 1, :, :, cols].reshape(2 * tok_dev, chunk)
            got = (weight_col * jnp.dot(pick, grads, preferred_element_type=F32)).astype(BF16)
            sg[g - 1, :, :, cols] = got.reshape(NX, 16, chunk)
            return carry

        lax.fori_loop(0, chunks, body, 0)

    def select_one(g, b, first, count):
        index_col, weight_col = columns_of(zm[pairs, b, pl.ds(z, 1), :])
        pick = one_hot(index_col, tok_dev)
        is_grad = jnp.broadcast_to(upper, (64, chunk)) > 0.0

        def body(n, carry):
            cols = pl.ds(pl.multiple_of(n * chunk, chunk), chunk)
            rows = jnp.dot(pick, zx[pairs, b, :, cols], preferred_element_type=F32)
            grads = weight_col * jnp.dot(pick, zc[pairs, b, :, cols], preferred_element_type=F32)
            sx[g, :, :, cols] = jnp.where(is_grad, grads, rows).astype(BF16).reshape(NX, 16, chunk)
            return carry

        lax.fori_loop(first, first + count, body, 0)

    xcp = {}
    x_far, x_next, x_prev = (x + 2) % NX, (x + 1) % NX, (x + 3) % NX

    def x_copy(i, g, src, dst, way):
        xcp[i, g] = send(src, dst, xs_sem.at[i, g], xr_sem.at[i, g], at_x(way))

    def x_stay(i, g, src, dst):
        xcp[i, g] = pltpu.make_async_copy(src, dst, xl_sem.at[i - 8, g])
        xcp[i, g].start()

    def is_pair(g):
        return 1 <= g <= pairs

    def send_rows(g):
        x_copy(0, g, sx.at[g, x_far], lx.at[g], 1)
        x_copy(2, g, sx.at[g, x_next], rx.at[g, 0, 1], 1)
        x_copy(3, g, sx.at[g, x_prev], rx.at[g, 0, 3], -1)
        x_stay(8, g, sx.at[g, x], rx.at[g, 0, 0])

    def send_grads(g):
        x_copy(1, g, sg.at[g - 1, x_far], lg.at[g - 1], -1)
        x_copy(5, g, sg.at[g - 1, x_prev], rg.at[g - 1, 0, 3], -1)
        x_copy(4, g, sg.at[g - 1, x_next], rg.at[g - 1, 0, 1], 1)
        x_stay(9, g, sg.at[g - 1, x], rg.at[g - 1, 0, 0])

    def send_left(g):
        x_copy(0, g, sx.at[g, x_far, :, left_half], lx.at[g, :, left_half], 1)
        x_copy(2, g, sx.at[g, x_next, :, left_half], rx.at[g, 0, 1, :, left_half], 1)
        x_copy(3, g, sx.at[g, x_prev, :, left_half], rx.at[g, 0, 3, :, left_half], -1)
        x_stay(8, g, sx.at[g, x, :, left_half], rx.at[g, 0, 0, :, left_half])

    def send_right(g):
        x_copy(1, g, sx.at[g, x_far, :, right_half], lx.at[g, :, right_half], -1)
        x_copy(5, g, sx.at[g, x_prev, :, right_half], rx.at[g, 0, 3, :, right_half], -1)
        x_copy(4, g, sx.at[g, x_next, :, right_half], rx.at[g, 0, 1, :, right_half], 1)
        x_stay(9, g, sx.at[g, x, :, right_half], rx.at[g, 0, 0, :, right_half])

    def is_pair(g):
        return 1 <= g <= pairs

    def relay_first(g):
        xcp[0, g].wait_recv()
        if is_pair(g):
            x_copy(6, g, lx.at[g], rx.at[g, 0, 2], 1)
        else:
            x_copy(6, g, lx.at[g, :, left_half], rx.at[g, 0, 2, :, left_half], 1)

    def relay_second(g):
        xcp[1, g].wait_recv()
        if is_pair(g):
            x_copy(7, g, lg.at[g - 1], rg.at[g - 1, 0, 2], -1)
        else:
            x_copy(7, g, lx.at[g, :, right_half], rx.at[g, 0, 2, :, right_half], -1)

    pcp = {}

    def share(i, g, buf, h, cols=slice(None)):
        pcp[i, g] = send(
            buf.at[h, 0, :, :, cols], buf.at[h, 1, :, :, cols], ps_sem.at[i, g], pr_sem.at[i, g], partner
        )

    def share_first(g):
        xcp[8, g].wait()
        for i in (2, 3, 6):
            xcp[i, g].wait_recv()
        if is_pair(g):
            share(0, g, rx, g)
        else:
            share(0, g, rx, g, left_half)

    def share_second(g):
        xcp[9, g].wait()
        for i in (4, 5, 7):
            xcp[i, g].wait_recv()
        if is_pair(g):
            share(1, g, rg, g - 1)
        else:
            share(1, g, rx, g, right_half)

    def arrived(g, n):
        for i in range(g, g + n):
            pcp[0, i].wait_recv()
            pcp[1, i].wait_recv()

    def times(lhs, rows):
        return lax.dot_general(lhs, rows, (((1,), (1,)), ((), ())), preferred_element_type=F32)

    def pointwise(g, at, width, single, qa, qb):
        def body(i, carry):
            q = qa + i // 2
            rows = pl.ds(pl.multiple_of((i % 2) * (hs // 2), hs // 2), hs // 2)
            pre_gate, pre_up, tan_gate, tan_up, back = [proj[q, k, rows, pl.ds(at, width)] for k in range(5)]
            if single:
                back = pltpu.roll(back, width - CAP, 1)
                is_row = (lax.broadcasted_iota(jnp.int32, (hs // 2, width), 1) // CAP) % 2 == 0
                back = jnp.where(is_row, back, 0.0)
            sig = 1.0 / (1.0 + jnp.exp(-pre_gate))
            first = sig * (1.0 + pre_gate * (1.0 - sig))
            second = sig * (1.0 - sig) * (2.0 + pre_gate * (1.0 - 2.0 * sig))
            cols = pl.ds(g * rows_of, width)
            dirs[q, 0, rows, cols] = (back * (tan_up * first + pre_up * second * tan_gate)).astype(BF16)
            dirs[q, 1, rows, cols] = (back * first * tan_gate).astype(BF16)
            return carry

        lax.fori_loop(0, 2 * (qb - qa), body, 0)

    def terms(g, n, qa, qb):
        width = n * rows_of
        slices = qb - qa

        got = times(wbuf[qa:qb, :4].reshape(slices * 4 * hs, dim), rx[g : g + n].reshape(width, dim))
        proj[qa:qb, :4, :, pl.ds(0, width)] = got.reshape(slices, 4, hs, width)
        down = wbuf[qa:qb, 4].reshape(slices * hs, dim)
        singles = 0 if is_pair(g) else rows_of
        if singles:
            got = times(down, rx[g].reshape(rows_of, dim))
            proj[qa:qb, 4, :, pl.ds(0, rows_of)] = got.reshape(slices, hs, rows_of)
            pointwise(g, 0, rows_of, True, qa, qb)
            g = g + 1
        rest = width - singles
        if rest:
            got = times(down, rg[g - 1 : g - 1 + rest // rows_of].reshape(rest, dim))
            proj[qa:qb, 4, :, pl.ds(singles, rest)] = got.reshape(slices, hs, rest)
            pointwise(g, singles, rest, False, qa, qb)

    def early_product(qa, qb, first, count, add):
        depth = count * rows_of
        slices = qb - qa
        wide = chunk if slices == 1 else chunk // 2

        def body(i, carry):
            cols = pl.ds(pl.multiple_of(i * wide, wide), wide)
            rows = rx[first : first + count, :, :, :, cols].reshape(depth, wide)
            d = dirs[qa:qb, :, :, pl.ds(first * rows_of, depth)].reshape(slices * 2 * hs, depth)
            value = jnp.dot(d, rows, preferred_element_type=F32).reshape(slices, 2, hs, wide)
            part[qa:qb, :, :, cols] = part[qa:qb, :, :, cols] + value if add else value
            return carry

        lax.fori_loop(0, dim // wide, body, 0)

    def last_product(q, first, count):
        depth = count * rows_of

        def body(n, carry):
            cols = pl.ds(pl.multiple_of(n * chunk, chunk), chunk)
            rows = rx[first : first + count, :, :, :, cols].reshape(depth, chunk)
            d = dirs[q, :, :, pl.ds(first * rows_of, depth)].reshape(2 * hs, depth)
            acc = part[q, :, :, cols] + jnp.dot(d, rows, preferred_element_type=F32).reshape(2, hs, chunk)
            gate, up = acc[0], acc[1]
            if q == QFAR:
                sb[0, :, cols] = gate.astype(BF16)
                sb[1, :, cols] = up.astype(BF16)
            elif q == QNEXT:
                part[q, 0, :, cols] = gate
                sb[2, :, cols] = up.astype(BF16)
            elif q == QPREV:
                sb[3, :, cols] = gate.astype(BF16)
                part[q, 1, :, cols] = up
            else:
                part[q, :, :, cols] = acc
            return carry

        lax.fori_loop(0, chunks, body, 0)

    rcp = {}

    def r_send(i, src, dst, way):
        rcp[i] = send(sb.at[src], dst, rs_sem.at[i], rr_sem.at[i], at_y(way))

    local[0].wait()
    local[1].wait()
    select_one(own, 0, 0, chunks)
    send_left(own)
    send_right(own)
    for s in range(1, steps):
        z_wait(tokens + tables, s)
        pick, weight_col = pick_of(s)
        select_rows(s, pick)
        send_rows(s)
        relay_first(s - 1)
        if s >= 2:
            share_first(s - 2)
        if s == steps - 2:
            y_near()
            arrived(own, 2)
            terms(own, 2, QNEXT, 4)
        if s == steps - 1:
            early_product(QNEXT, 4, own, 4, False)
        z_wait(cotangents, s)
        select_grads(s, pick, weight_col)
        send_grads(s)
        relay_second(s - 1)
        if s >= 2:
            share_second(s - 2)
        if s == 3:
            y_forward()
        if s == steps - 2:
            arrived(2, 2)
            terms(2, 2, QNEXT, 4)
    arrived(4, 2)
    terms(4, 2, QNEXT, 4)
    z_wait(far_lanes[1] + far_lanes[0], steps)
    select_one(far, 1, 0, chunks // 2)
    send_left(far)
    relay_first(pairs)
    share_first(pairs - 1)
    z_wait(far_lanes[2], steps)
    select_one(far, 1, chunks // 2, chunks // 2)
    send_right(far)
    relay_second(pairs)
    share_second(pairs - 1)
    y_finish()
    for g in (own, 2):
        terms(g, 2, QFAR, QNEXT)
    relay_first(far)
    terms(4, 2, QFAR, QNEXT)
    relay_second(far)
    share_first(pairs)
    share_second(pairs)
    early_product(QFAR, QNEXT, own, 6, False)
    early_product(QNEXT, 4, 4, 2, True)
    arrived(6, 2)
    share_first(far)
    terms(6, 2, QFAR, QNEXT)
    share_second(far)
    terms(6, 2, QNEXT, QPREV)
    arrived(far, 1)
    terms(far, 1, QFAR, QNEXT)
    last_product(QFAR, 6, 3)
    r_send(0, 0, rb.at[0], 1)
    r_send(1, 1, rb.at[1], -1)
    terms(6, 2, QPREV, 4)
    terms(far, 1, QNEXT, 4)
    last_product(QNEXT, 6, 3)
    r_send(2, 2, theirs_hbm.at[0, 0, 1], 1)
    last_product(QPREV, 6, 3)
    r_send(3, 3, theirs_hbm.at[1, 0, 0], -1)
    last_product(QOWN, 6, 3)
    keep = pltpu.make_async_copy(part.at[QOWN], mine_hbm.at[0], loc_sem.at[0])
    keep.start()
    rcp[0].wait_recv()
    sb[4] = (part[QNEXT, 0] + rb[0].astype(F32)).astype(BF16)
    r_send(4, 4, theirs_hbm.at[0, 0, 0], 1)
    rcp[1].wait_recv()
    sb[5] = (part[QPREV, 1] + rb[1].astype(F32)).astype(BF16)
    r_send(5, 5, theirs_hbm.at[1, 0, 1], -1)
    keep.wait()
    for i in range(2, 6):
        rcp[i].wait_recv()
    for c in sent:
        c.wait_send()


def local(tokens, cotangent, routes, combine, w_in, w_out, v_in):
    nz = lax.axis_size("expert") // NX
    pairs = nz // 2 - 1
    groups = pairs + 2
    tok_dev, dim = tokens.shape
    hs = w_out.shape[1]
    top = routes.shape[1]
    rows_of = 2 * NX * 16
    any_spec = pl.BlockSpec(memory_space=pl.ANY)
    dma = pltpu.SemaphoreType.DMA
    mine, theirs = pl.pallas_call(
        functools.partial(kernel, nz),
        out_shape=(
            jax.ShapeDtypeStruct((1, 2, hs, dim), F32),
            jax.ShapeDtypeStruct((2, 1, 2, hs, dim), BF16),
        ),
        in_specs=[pl.BlockSpec(memory_space=pltpu.HBM)] * 7,
        out_specs=(any_spec, any_spec),
        scratch_shapes=[
            pltpu.VMEM((top, tok_dev), jnp.int32),
            pltpu.VMEM((top, tok_dev), F32),
            pltpu.VMEM((pairs + 1, 2, tok_dev, dim), BF16),
            pltpu.VMEM((pairs + 1, 2, tok_dev, dim), BF16),
            pltpu.VMEM((pairs + 1, 2, nz, 128), F32),
            pltpu.VMEM((groups, NX, 16, dim), BF16),
            pltpu.VMEM((pairs, NX, 16, dim), BF16),
            pltpu.VMEM((groups, 16, dim), BF16),
            pltpu.VMEM((pairs, 16, dim), BF16),
            pltpu.VMEM((groups, 2, NX, 16, dim), BF16),
            pltpu.VMEM((pairs, 2, NX, 16, dim), BF16),
            pltpu.VMEM((4, 5, hs, dim), BF16),
            pltpu.VMEM((4, 5, hs, 2 * rows_of), F32),
            pltpu.VMEM((4, 2, hs, groups * rows_of), BF16),
            pltpu.VMEM((4, 2, hs, dim), F32),
            pltpu.VMEM((6, hs, dim), BF16),
            pltpu.VMEM((2, hs, dim), BF16),
            dma((7,)),
            dma((2, 4, pairs + 1)),
            dma((2, 4, pairs + 1)),
            dma((2, 6)),
            dma((2, 6)),
            dma((8, groups)),
            dma((8, groups)),
            dma((2, groups)),
            dma((2, groups)),
            dma((2, groups)),
            dma((6,)),
            dma((6,)),
        ],
        compiler_params=pltpu.CompilerParams(
            collective_id=0, has_side_effects=True, vmem_limit_bytes=50 * 1024 * 1024
        ),
    )(*[pltpu.with_memory_space_constraint(v, pltpu.HBM) for v in (tokens, cotangent, routes.T, combine.T, w_in, w_out, v_in)])
    return mine + theirs[0].astype(F32) + theirs[1].astype(F32)


def solution(mesh):
    in_specs = (
        P(("dp", "expert"), None),
        P(("dp", "expert"), None),
        P(("dp", "expert"), None),
        P(("dp", "expert"), None),
        P("expert", None, "dp", None),
        P("expert", "dp", None),
        P("expert", None, "dp", None),
    )
    out_specs = P("expert", None, "dp", None)
    return jax.shard_map(local, mesh=mesh, in_specs=in_specs, out_specs=out_specs, check_vma=False)
```
